32 devices in a mesh: groups: 2 (over x), seq: 16 (over z, y, core).
Axes of the slice: x: 2, y: 2, z: 4, core: 2. Of those that a mesh axis runs over, the one named last changes fastest.
Arguments:
- queries: bfloat16 [8192, 2048], P(('groups', 'seq')), parts along dimension 0, may hold values from -6 to 6
- keys: bfloat16 [8192, 2048], P(('groups', 'seq')), parts along dimension 0, may hold values from -6 to 6
- values: bfloat16 [8192, 2048], P(('groups', 'seq')), parts along dimension 0, may hold values from -6 to 6
- gain: float32 [2048], replicated, may hold values from 0.1 to 1.9
Outputs:
- attended: bfloat16 [8192, 2048], P(('groups', 'seq')), parts along dimension 0
The draws below stay inside these ranges and needn't reach their ends.
There are 2 independent parts, one for each index of `groups`. The reference program is written for one: setup_inputs(seed, part) draws one part's arguments, and reference() takes and returns one part's arrays. A program takes and returns all parts, laid end to end along the dimension named above; an argument that names none is the same for every part. Nothing has to cross between parts.
All inputs are finite; a program needn't handle non-finite values.
Results may differ from the reference program's by a relative error of at most 0.01.
Values may be sent and summed in bfloat16 or wider, within the bound.
No kernel may reach another device: no remote copies, remote signals or barrier semaphores. Data moves between devices by JAX's collectives and lax.ppermute only.
A program may use at most 192 MiB of HBM per device.

```python
import jax
import jax.numpy as jnp
from jax import lax

HEADS = 32
HEAD_DIM = 64
D = 2048
TOK_DEV = 256
SEQ = 4096
N_SEQ = 16


def block_levels(key, shape, shards, smallest, largest):
    level = 1.0
    for dim, parts in shards:
        draws = jax.random.uniform(jax.random.fold_in(jax.random.fold_in(key, 6), dim), (parts,), jnp.float32, smallest / len(shards), largest / len(shards))
        level = level * jnp.repeat(jnp.exp(draws), shape[dim] // parts).reshape((-1,) + (1,) * (len(shape) - 1 - dim))
    return level


def gaussian(rng, extent, width, bound, shards=(), held_as=jnp.bfloat16):
    result = width * jax.random.normal(rng, extent, jnp.float32)
    if shards:
        result = result * block_levels(rng, extent, shards, -0.22, 0.18)
    return jnp.clip(result, -bound, bound).astype(held_as)


def setup_inputs(seed: int = 0, part: int = 0) -> dict:
    key_list = jax.random.split(jax.random.key(seed), 5)
    own_keys = jax.random.split(jax.random.fold_in(key_list[4], part), 5)
    queries = gaussian(own_keys[0], (SEQ, D), 1.0, 6.0, ((0, 16),))
    keys = gaussian(own_keys[1], (SEQ, D), 1.0, 6.0, ((0, 16),))
    values = gaussian(own_keys[2], (SEQ, D), 1.0, 6.0, ((0, 16),))
    gain = jnp.clip(1.0 + 0.18 * jax.random.normal(key_list[3], (D,), jnp.float32), 0.1, 1.9)
    return {"queries": queries, "keys": keys, "values": values, "gain": gain}


def block_out(fq, fk, vals, prior):
    prior_b = prior.astype(jnp.bfloat16).astype(jnp.float32)
    fq32 = fq.astype(jnp.float32)
    fk32 = fk.astype(jnp.float32)
    v32 = vals.astype(jnp.float32)
    count = fq.shape[0]
    scores = jnp.einsum('thd,shd->hts', fq32, fk32)
    rows = jnp.arange(count)[:, None]
    cols = jnp.arange(count)[None, :]
    scores = jnp.where(cols <= rows, scores, 0.0).astype(jnp.bfloat16).astype(jnp.float32)
    intra = jnp.einsum('hts,she->the', scores, v32)
    inter = jnp.einsum('thd,hde->the', fq32, prior_b)
    return inter + intra

def reference(queries, keys, values, gain):
    blocks = N_SEQ
    fq = jax.nn.relu(queries).reshape(blocks, TOK_DEV, HEADS, HEAD_DIM)
    fk = jax.nn.relu(keys).reshape(blocks, TOK_DEV, HEADS, HEAD_DIM)
    vals = values.reshape(blocks, TOK_DEV, HEADS, HEAD_DIM)

    def step(prior, item):
        q_blk, k_blk, v_blk = item
        numer = block_out(q_blk, k_blk, v_blk, prior)
        state = jnp.einsum('thd,the->hde', k_blk.astype(jnp.float32), v_blk.astype(jnp.float32))
        return (prior + state, numer)
    init = jnp.zeros((HEADS, HEAD_DIM, HEAD_DIM), jnp.float32)
    final, numer = lax.scan(step, init, (fq, fk, vals))
    mean_sq = lax.optimization_barrier(jnp.mean(numer * numer, axis=-1, keepdims=True))
    normed = numer * lax.rsqrt(mean_sq + 1e-05)
    normed = normed.reshape(blocks * TOK_DEV, HEADS * HEAD_DIM) * gain[None, :]
    return normed.astype(jnp.bfloat16)
```

```python
import functools

import jax
import jax.numpy as jnp
from jax import lax
from jax.experimental import pallas as pl
from jax.experimental.pallas import tpu as pltpu
from jax.sharding import PartitionSpec as P


HEAD_DIM = 64
PAIR = 2 * HEAD_DIM
QUAD = 4 * HEAD_DIM
EPS = 1e-05
AXIS = "seq"


def swap_with(x, bit, size):
    return lax.ppermute(x, AXIS, [(i, i ^ bit) for i in range(size)])


def first_lanes(shape):
    return lax.broadcasted_iota(jnp.int32, shape, len(shape) - 1) % PAIR < HEAD_DIM


def dot(a, b, dims):
    return lax.dot_general(a, b, (dims, ((), ())), preferred_element_type=jnp.float32)


def state_kernel(k_hbm, v_hbm, send_ref, keep_ref, k_ref, v_ref, sems):
    half = k_ref.shape[1] // 2
    core = lax.axis_index(AXIS) % 2
    copies = []
    for step in range(2):
        which = 1 - core if step == 0 else core
        lanes = pl.ds(pl.multiple_of(which * half, half), half)
        here = pl.ds(step * half, half)
        pair = [
            pltpu.make_async_copy(src.at[:, lanes], dst.at[:, here], sems.at[step, n])
            for n, (src, dst) in enumerate(((k_hbm, k_ref), (v_hbm, v_ref)))
        ]
        for copy in pair:
            copy.start()
        copies.append(pair)
    first = first_lanes((HEAD_DIM, PAIR))
    for step in range(2):
        for copy in copies[step]:
            copy.wait()
        for quad in range(half // QUAD):
            lanes = pl.ds(step * half + quad * QUAD, QUAD)
            fk = jnp.maximum(k_ref[:, lanes], 0)
            full = dot(fk, v_ref[:, lanes], ((0,), (0,)))
            for p in range(2):
                at = p * PAIR
                rows = full[at : at + PAIR, at : at + PAIR]
                packed = jnp.where(first, rows[:HEAD_DIM], rows[HEAD_DIM:])
                to = pl.ds((quad * 2 + p) * HEAD_DIM, HEAD_DIM)
                if step == 0:
                    send_ref[to, :] = packed.astype(jnp.bfloat16)
                else:
                    keep_ref[to, :] = packed


def intra_kernel(q_hbm, k_ref, v_ref, fq_ref, intra_ref, q_buf, sem, *, part):
    count, width = fq_ref.shape
    half = k_ref.shape[1] // 2
    core = lax.axis_index(AXIS) % 2
    which = 1 - core if part < 2 else core
    start = pl.multiple_of(which * half + (part % 2) * width, width)
    copy = pltpu.make_async_copy(q_hbm.at[:, pl.ds(start, width)], q_buf, sem)
    copy.start()
    copy.wait()
    mid = count // 2
    first = first_lanes((count, PAIR))
    rows = lax.broadcasted_iota(jnp.int32, (mid, mid), 0)
    cols = lax.broadcasted_iota(jnp.int32, (mid, mid), 1)
    causal = cols <= rows
    for p in range(width // PAIR):
        lanes = pl.ds(p * PAIR, PAIR)
        there = pl.ds(part * width + p * PAIR, PAIR)
        fq = jnp.maximum(q_buf[:, lanes], 0)
        fq_ref[:, lanes] = fq
        fk = jnp.maximum(k_ref[:, there], 0)
        val = v_ref[:, there]
        zero = jnp.zeros_like(fq)
        top, low, weights = [], [], []
        for h in range(2):
            mine = first if h == 0 else jnp.logical_not(first)
            mine_q = jnp.where(mine, fq, zero)
            s_top = dot(mine_q[:mid], fk[:mid], ((1,), (1,)))
            s_low = dot(mine_q[mid:], fk, ((1,), (1,)))
            s_top = jnp.where(causal, s_top, 0.0).astype(jnp.bfloat16)
            s_diag = jnp.where(causal, s_low[:, mid:], 0.0).astype(jnp.bfloat16)
            s_low = jnp.concatenate([s_low[:, :mid].astype(jnp.bfloat16), s_diag], axis=1)
            mine_v = jnp.where(mine, val, zero)
            top.append(s_top)
            low.append(s_low)
            weights.append(mine_v)
        w_top = jnp.concatenate([w[:mid] for w in weights], axis=0)
        intra_ref[:mid, lanes] = dot(jnp.concatenate(top, axis=1), w_top, ((1,), (0,)))
        w_low = jnp.concatenate(weights, axis=0)
        intra_ref[mid:, lanes] = dot(jnp.concatenate(low, axis=1), w_low, ((1,), (0,)))


def final_kernel(prior_ref, fq0, fq1, in0, in1, gain_ref, *rest, step):
    out_hbm, out_buf, sems = rest[-3:]
    half = out_buf.shape[1]
    width = fq0.shape[1]
    core = lax.axis_index(AXIS) % 2
    which = core if step == 0 else 1 - core
    base = pl.multiple_of(which * half, half)
    lane = lax.broadcasted_iota(jnp.int32, (QUAD, QUAD), 1) // HEAD_DIM
    row = lax.broadcasted_iota(jnp.int32, (QUAD, QUAD), 0) // HEAD_DIM
    same = lane == row
    ones = jnp.where(same, 1.0 / HEAD_DIM, 0.0).astype(jnp.bfloat16)
    copies = []
    for quad in range(half // QUAD):
        fq_ref, intra_ref = (fq0, in0) if quad * QUAD < width else (fq1, in1)
        lanes = pl.ds(quad * QUAD % width, QUAD)
        one = prior_ref[pl.ds(quad * PAIR, HEAD_DIM), :]
        two = prior_ref[pl.ds(quad * PAIR + HEAD_DIM, HEAD_DIM), :]
        wide = jnp.concatenate([one, two], axis=1)
        block = jnp.concatenate([wide] * 4, axis=0)
        block = jnp.where(same, block, jnp.zeros_like(block))
        numer = dot(fq_ref[:, lanes], block, ((1,), (0,))) + intra_ref[:, lanes]
        square = (numer * numer).astype(jnp.bfloat16)
        mean_sq = dot(square, ones, ((1,), (0,)))
        gain = gain_ref[:, pl.ds(pl.multiple_of(base + quad * QUAD, QUAD), QUAD)]
        normed = numer * lax.rsqrt(mean_sq + EPS) * gain
        out_buf[:, pl.ds(quad * QUAD, QUAD)] = normed.astype(jnp.bfloat16)
        copy = pltpu.make_async_copy(
            out_buf.at[:, pl.ds(quad * QUAD, QUAD)],
            out_hbm.at[:, pl.ds(pl.multiple_of(base + quad * QUAD, QUAD), QUAD)],
            sems.at[quad],
        )
        copy.start()
        copies.append(copy)
    for copy in copies:
        copy.wait()


ANY = pl.BlockSpec(memory_space=pl.ANY)
VMEM = pl.BlockSpec(memory_space=pltpu.VMEM)


def on_device(queries, keys, values, gain, *, size):
    count, width = queries.shape
    half, part = width // 2, width // 4
    rows = half // PAIR * HEAD_DIM
    bf16, f32 = jnp.bfloat16, jnp.float32
    here = lax.axis_index(AXIS)

    stay = lambda x: pltpu.with_memory_space_constraint(x, pltpu.VMEM)
    send, keep, k_vmem, v_vmem = pl.pallas_call(
        state_kernel,
        out_shape=(
            pltpu.VMEM((rows, PAIR), bf16),
            pltpu.VMEM((rows, PAIR), f32),
            pltpu.VMEM((count, width), bf16),
            pltpu.VMEM((count, width), bf16),
        ),
        in_specs=[ANY, ANY],
        out_specs=(VMEM, VMEM, VMEM, VMEM),
        scratch_shapes=[pltpu.SemaphoreType.DMA((2, 2))],
        name="state",
    )(keys, values)

    parts = []
    for n in range(4):
      parts.append(
          pl.pallas_call(
              functools.partial(intra_kernel, part=n),
              out_shape=(pltpu.VMEM((count, part), bf16), pltpu.VMEM((count, part), f32)),
              in_specs=[ANY, VMEM, VMEM],
              out_specs=(VMEM, VMEM),
              scratch_shapes=[pltpu.VMEM((count, part), bf16), pltpu.SemaphoreType.DMA],
              cost_estimate=pl.CostEstimate(flops=150_000_000, transcendentals=0, bytes_accessed=1_500_000),
          )(queries, stay(k_vmem), stay(v_vmem))
      )

    core, side = here % 2, here // 2 % 2
    got_core = swap_with(send, 1, size).astype(f32)
    chip = keep + got_core
    q_rows = rows // 2
    low, high = chip[:q_rows], chip[q_rows:]
    own = jnp.where(side == 0, low, high)
    other = jnp.where(side == 0, high, low)
    got_side = swap_with(other.astype(bf16), 2, size).astype(f32)
    total = own + got_side
    before = jnp.zeros_like(total)
    bit = 4
    while bit < size:
        got = swap_with(total.astype(bf16), bit, size).astype(f32)
        before = before + jnp.where(here // bit % 2 == 1, got, 0.0)
        total = total + got
        bit *= 2
    to_side = before + jnp.where(side == 0, own, 0.0)
    mine = before + jnp.where(side == 0, 0.0, got_side)
    got_base = swap_with(to_side.astype(bf16), 2, size).astype(f32)
    base = jnp.concatenate([jnp.where(side == 0, mine, got_base), jnp.where(side == 0, got_base, mine)], axis=0)
    to_core = base + jnp.where(core == 0, keep, 0.0)
    mine = (base + jnp.where(core == 0, 0.0, got_core)).astype(bf16)
    theirs = swap_with(to_core.astype(bf16), 1, size)

    gain2 = gain[None, :]
    out = None
    for step, prior in ((0, mine), (1, theirs)):
        (fq0, in0), (fq1, in1) = parts[2:] if step == 0 else parts[:2]
        args = [stay(prior), stay(fq0), stay(fq1), stay(in0), stay(in1), gain2]
        specs = [VMEM] * 6
        alias = {}
        if out is not None:
            args.append(out)
            specs.append(ANY)
            alias = {6: 0}
        out = pl.pallas_call(
            functools.partial(final_kernel, step=step),
            out_shape=jax.ShapeDtypeStruct((count, width), bf16),
            in_specs=specs,
            out_specs=ANY,
            scratch_shapes=[pltpu.VMEM((count, half), bf16), pltpu.SemaphoreType.DMA((half // QUAD,))],
            input_output_aliases=alias,
            cost_estimate=pl.CostEstimate(flops=100_000_000, transcendentals=0, bytes_accessed=2_000_000),
        )(*args)
    return out


def solution(mesh):
    return jax.shard_map(
        functools.partial(on_device, size=mesh.shape[AXIS]),
        mesh=mesh,
        in_specs=(
            P(("groups", "seq"), None),
            P(("groups", "seq"), None),
            P(("groups", "seq"), None),
            P(),
        ),
        out_specs=P(("groups", "seq"), None),
        check_vma=False,
    )
```

```python
import functools

import jax
import jax.numpy as jnp
from jax import lax
from jax.experimental import pallas as pl
from jax.experimental.pallas import tpu as pltpu
from jax.sharding import PartitionSpec as P


HEAD_DIM = 64
PAIR = 2 * HEAD_DIM
QUAD = 4 * HEAD_DIM
EPS = 1e-05
AXIS = "seq"


def swap_with(x, bit, size):
    return lax.ppermute(x, AXIS, [(i, i ^ bit) for i in range(size)])


def first_lanes(shape):
    return lax.broadcasted_iota(jnp.int32, shape, len(shape) - 1) % PAIR < HEAD_DIM


def dot(a, b, dims):
    return lax.dot_general(a, b, (dims, ((), ())), preferred_element_type=jnp.float32)


def state_kernel(k_hbm, v_hbm, send_ref, keep_ref, k_ref, v_ref, sems):
    half = k_ref.shape[1] // 2
    core = lax.axis_index(AXIS) % 2
    copies = []
    for step in range(2):
        which = 1 - core if step == 0 else core
        lanes = pl.ds(pl.multiple_of(which * half, half), half)
        here = pl.ds(step * half, half)
        pair = [
            pltpu.make_async_copy(src.at[:, lanes], dst.at[:, here], sems.at[step, n])
            for n, (src, dst) in enumerate(((k_hbm, k_ref), (v_hbm, v_ref)))
        ]
        for copy in pair:
            copy.start()
        copies.append(pair)
    first = first_lanes((HEAD_DIM, PAIR))
    for step in range(2):
        for copy in copies[step]:
            copy.wait()
        for quad in range(half // QUAD):
            lanes = pl.ds(step * half + quad * QUAD, QUAD)
            fk = jnp.maximum(k_ref[:, lanes], 0)
            full = dot(fk, v_ref[:, lanes], ((0,), (0,)))
            for p in range(2):
                at = p * PAIR
                rows = full[at : at + PAIR, at : at + PAIR]
                packed = jnp.where(first, rows[:HEAD_DIM], rows[HEAD_DIM:])
                to = pl.ds((quad * 2 + p) * HEAD_DIM, HEAD_DIM)
                if step == 0:
                    send_ref[to, :] = packed.astype(jnp.bfloat16)
                else:
                    keep_ref[to, :] = packed


def intra_kernel(q_hbm, k_ref, v_ref, out, q_buf, intra_ref, sems, *, part):
    count, width = q_buf.shape
    half = k_ref.shape[1] // 2
    core = lax.axis_index(AXIS) % 2
    which = 1 - core if part < 2 else core
    start = pl.multiple_of(which * half + (part % 2) * width, width)
    copy = pltpu.make_async_copy(q_hbm.at[:, pl.ds(start, width)], q_buf, sems.at[0])
    copy.start()
    copy.wait()
    copies = []
    mid = count // 2
    first = first_lanes((count, PAIR))
    rows = lax.broadcasted_iota(jnp.int32, (mid, mid), 0)
    cols = lax.broadcasted_iota(jnp.int32, (mid, mid), 1)
    causal = cols <= rows
    for p in range(width // PAIR):
        lanes = pl.ds(p * PAIR, PAIR)
        there = pl.ds(part * width + p * PAIR, PAIR)
        fq = jnp.maximum(q_buf[:, lanes], 0)
        fk = jnp.maximum(k_ref[:, there], 0)
        val = v_ref[:, there]
        zero = jnp.zeros_like(fq)
        top, low, weights = [], [], []
        for h in range(2):
            mine = first if h == 0 else jnp.logical_not(first)
            mine_q = jnp.where(mine, fq, zero)
            s_top = dot(mine_q[:mid], fk[:mid], ((1,), (1,)))
            s_low = dot(mine_q[mid:], fk, ((1,), (1,)))
            s_top = jnp.where(causal, s_top, 0.0).astype(jnp.bfloat16)
            s_diag = jnp.where(causal, s_low[:, mid:], 0.0).astype(jnp.bfloat16)
            s_low = jnp.concatenate([s_low[:, :mid].astype(jnp.bfloat16), s_diag], axis=1)
            mine_v = jnp.where(mine, val, zero)
            top.append(s_top)
            low.append(s_low)
            weights.append(mine_v)
        w_top = jnp.concatenate([w[:mid] for w in weights], axis=0)
        intra_ref[:mid, lanes] = dot(jnp.concatenate(top, axis=1), w_top, ((1,), (0,)))
        w_low = jnp.concatenate(weights, axis=0)
        intra_ref[mid:, lanes] = dot(jnp.concatenate(low, axis=1), w_low, ((1,), (0,)))
        copies.append(pltpu.make_async_copy(intra_ref.at[:, lanes], out.at[:, lanes], sems.at[p + 1]))
        copies[-1].start()
    for copy in copies:
        copy.wait()


def final_kernel(prior_ref, q_hbm, in0, in1, gain_ref, *rest, step):
    out_hbm, q_buf, in_buf, out_buf, q_sem, in_sems, sems = rest[-7:]
    half = out_buf.shape[1]
    width = half // 2
    core = lax.axis_index(AXIS) % 2
    which = core if step == 0 else 1 - core
    base = pl.multiple_of(which * half, half)
    loads = [pltpu.make_async_copy(q_hbm.at[:, pl.ds(base, half)], q_buf, q_sem)]
    for n, src in enumerate((in0, in1)):
        loads.append(pltpu.make_async_copy(src, in_buf.at[:, pl.ds(n * width, width)], in_sems.at[n]))
    for load in loads:
        load.start()
    lane = lax.broadcasted_iota(jnp.int32, (QUAD, QUAD), 1) // HEAD_DIM
    row = lax.broadcasted_iota(jnp.int32, (QUAD, QUAD), 0) // HEAD_DIM
    same = lane == row
    ones = jnp.where(same, 1.0 / HEAD_DIM, 0.0).astype(jnp.bfloat16)
    copies = []
    for quad in range(half // QUAD):
        lanes = pl.ds(quad * QUAD, QUAD)
        one = prior_ref[pl.ds(quad * PAIR, HEAD_DIM), :]
        two = prior_ref[pl.ds(quad * PAIR + HEAD_DIM, HEAD_DIM), :]
        wide = jnp.concatenate([one, two], axis=1)
        block = jnp.concatenate([wide] * 4, axis=0)
        block = jnp.where(same, block, jnp.zeros_like(block))
        if quad == 0:
            loads[0].wait()
        fq = jnp.maximum(q_buf[:, lanes], 0)
        if quad * QUAD % width == 0:
            loads[1 + quad * QUAD // width].wait()
        numer = dot(fq, block, ((1,), (0,))) + in_buf[:, lanes]
        square = (numer * numer).astype(jnp.bfloat16)
        mean_sq = dot(square, ones, ((1,), (0,)))
        there = pl.ds(pl.multiple_of(base + quad * QUAD, QUAD), QUAD)
        normed = numer * lax.rsqrt(mean_sq + EPS) * gain_ref[:, there]
        out_buf[:, lanes] = normed.astype(jnp.bfloat16)
        copy = pltpu.make_async_copy(out_buf.at[:, lanes], out_hbm.at[:, there], sems.at[quad])
        copy.start()
        copies.append(copy)
    for copy in copies:
        copy.wait()


PARAMS = pltpu.CompilerParams(vmem_limit_bytes=12 * 2**20)
ANY = pl.BlockSpec(memory_space=pl.ANY)
VMEM = pl.BlockSpec(memory_space=pltpu.VMEM)


def on_device(queries, keys, values, gain, *, size):
    count, width = queries.shape
    half, part = width // 2, width // 4
    rows = half // PAIR * HEAD_DIM
    bf16, f32 = jnp.bfloat16, jnp.float32
    here = lax.axis_index(AXIS)

    stay = lambda x: pltpu.with_memory_space_constraint(x, pltpu.VMEM)
    send, keep, k_vmem, v_vmem = pl.pallas_call(
        state_kernel,
        out_shape=(
            pltpu.VMEM((rows, PAIR), bf16),
            pltpu.VMEM((rows, PAIR), f32),
            pltpu.VMEM((count, width), bf16),
            pltpu.VMEM((count, width), bf16),
        ),
        in_specs=[ANY, ANY],
        out_specs=(VMEM, VMEM, VMEM, VMEM),
        scratch_shapes=[pltpu.SemaphoreType.DMA((2, 2))],
        compiler_params=PARAMS,
        name="state",
    )(keys, values)

    parts = []
    for n in range(4):
      parts.append(
          pl.pallas_call(
              functools.partial(intra_kernel, part=n),
              out_shape=jax.ShapeDtypeStruct((count, part), f32),
              in_specs=[ANY, VMEM, VMEM],
              out_specs=ANY,
              scratch_shapes=[
                  pltpu.VMEM((count, part), bf16),
                  pltpu.VMEM((count, part), f32),
                  pltpu.SemaphoreType.DMA((1 + part // PAIR,)),
              ],
              cost_estimate=pl.CostEstimate(flops=150_000_000, transcendentals=0, bytes_accessed=1_500_000),
              compiler_params=PARAMS,
          )(queries, stay(k_vmem), stay(v_vmem))
      )

    core, side = here % 2, here // 2 % 2
    got_core = swap_with(send, 1, size).astype(f32)
    chip = keep + got_core
    q_rows = rows // 2
    low, high = chip[:q_rows], chip[q_rows:]
    own = jnp.where(side == 0, low, high)
    other = jnp.where(side == 0, high, low)
    got_side = swap_with(other.astype(bf16), 2, size).astype(f32)
    total = own + got_side
    before = jnp.zeros_like(total)
    bit = 4
    while bit < size:
        got = swap_with(total.astype(bf16), bit, size).astype(f32)
        before = before + jnp.where(here // bit % 2 == 1, got, 0.0)
        total = total + got
        bit *= 2
    to_side = before + jnp.where(side == 0, own, 0.0)
    mine = before + jnp.where(side == 0, 0.0, got_side)
    got_base = swap_with(to_side.astype(bf16), 2, size).astype(f32)
    base = jnp.concatenate([jnp.where(side == 0, mine, got_base), jnp.where(side == 0, got_base, mine)], axis=0)
    to_core = base + jnp.where(core == 0, keep, 0.0)
    mine = (base + jnp.where(core == 0, 0.0, got_core)).astype(bf16)
    theirs = swap_with(to_core.astype(bf16), 1, size)

    gain2 = gain[None, :]
    out = None
    for step, prior in ((0, mine), (1, theirs)):
        args = [prior, queries, *(parts[2:] if step == 0 else parts[:2]), gain2]
        specs = [VMEM, ANY, ANY, ANY, VMEM]
        alias = {}
        if out is not None:
            args.append(out)
            specs.append(ANY)
            alias = {5: 0}
        out = pl.pallas_call(
            functools.partial(final_kernel, step=step),
            out_shape=jax.ShapeDtypeStruct((count, width), bf16),
            in_specs=specs,
            out_specs=ANY,
            scratch_shapes=[
                pltpu.VMEM((count, half), bf16),
                pltpu.VMEM((count, half), f32),
                pltpu.VMEM((count, half), bf16),
                pltpu.SemaphoreType.DMA,
                pltpu.SemaphoreType.DMA((2,)),
                pltpu.SemaphoreType.DMA((half // QUAD,)),
            ],
            input_output_aliases=alias,
            cost_estimate=pl.CostEstimate(flops=100_000_000, transcendentals=0, bytes_accessed=2_000_000),
            compiler_params=PARAMS,
        )(*args)
    return out


def solution(mesh):
    return jax.shard_map(
        functools.partial(on_device, size=mesh.shape[AXIS]),
        mesh=mesh,
        in_specs=(
            P(("groups", "seq"), None),
            P(("groups", "seq"), None),
            P(("groups", "seq"), None),
            P(),
        ),
        out_specs=P(("groups", "seq"), None),
        check_vma=False,
    )
```

```python
import functools

import jax
import jax.numpy as jnp
from jax import lax
from jax.experimental import pallas as pl
from jax.experimental.pallas import tpu as pltpu
from jax.sharding import PartitionSpec as P


HEAD_DIM = 64
PAIR = 2 * HEAD_DIM
QUAD = 4 * HEAD_DIM
EPS = 1e-05
AXIS = "seq"
BF16, F32 = jnp.bfloat16, jnp.float32


def core_bit():
    return lax.axis_index(AXIS) & 1


def side_bit():
    return (lax.axis_index(AXIS) >> 1) & 1


def aligned(index, by):
    return pl.multiple_of(index * by, by)


def first_lanes(shape):
    return lax.broadcasted_iota(jnp.int32, shape, len(shape) - 1) % PAIR < HEAD_DIM


def dot(a, b, dims):
    return lax.dot_general(a, b, (dims, ((), ())), preferred_element_type=F32)


def states_of(k_ref, v_ref, out_ref, start, width):
    first = first_lanes((HEAD_DIM, PAIR))
    for quad in range(width // QUAD):
        lanes = pl.ds(start + quad * QUAD, QUAD)
        fk = jnp.maximum(k_ref[:, lanes], 0)
        full = dot(fk, v_ref[:, lanes], ((0,), (0,)))
        for p in range(2):
            at = p * PAIR
            rows = full[at : at + PAIR, at : at + PAIR]
            packed = jnp.where(first, rows[:HEAD_DIM], rows[HEAD_DIM:])
            out_ref[pl.ds((quad * 2 + p) * HEAD_DIM, HEAD_DIM), :] = packed.astype(out_ref.dtype)


def send_kernel(k_hbm, v_hbm, send_ref, k_ref, v_ref, sems):
    half = k_ref.shape[1] // 2
    core = core_bit()
    loads = []
    for step, which in enumerate((1 - core, core)):
        for n, (src, dst) in enumerate(((k_hbm, k_ref), (v_hbm, v_ref))):
            there, here = pl.ds(aligned(which, half), half), pl.ds(step * half, half)
            loads.append(pltpu.make_async_copy(src.at[:, there], dst.at[:, here], sems.at[step, n]))
            loads[-1].start()
    loads[0].wait()
    loads[1].wait()
    states_of(k_ref, v_ref, send_ref, 0, half)
    loads[2].wait()
    loads[3].wait()


def keep_kernel(k_ref, v_ref, q_hbm, keep_ref, q_ref, sems):
    half = k_ref.shape[1] // 2
    core = core_bit()
    loads = []
    for step, which in enumerate((1 - core, core)):
        there, here = pl.ds(aligned(which, half), half), pl.ds(step * half, half)
        loads.append(pltpu.make_async_copy(q_hbm.at[:, there], q_ref.at[:, here], sems.at[step]))
        loads[-1].start()
    states_of(k_ref, v_ref, keep_ref, half, half)
    for load in loads:
        load.wait()


def after_core(keep, got, send, own, ext):
    rows = own.shape[0]
    side = side_bit()
    mine, other = pl.ds(aligned(side, rows), rows), pl.ds(aligned(1 - side, rows), rows)
    send[...] = (keep[other, :] + got[other, :].astype(F32)).astype(BF16)
    own[...] = keep[mine, :] + got[mine, :].astype(F32)

    @pl.when(core_bit() == 0)
    def _():
        ext[...] = keep[...]

    @pl.when(core_bit() == 1)
    def _():
        ext[...] = got[...].astype(F32)


def after_side(own, got, send, total, ext):
    value = own[...] + got[...].astype(F32)
    send[...] = value.astype(BF16)
    total[...] = value
    ext[...] = jnp.where(side_bit() == 0, own[...], got[...].astype(F32))


def after_outer(total, before, got, send, total_out, before_out, *, level):
    value = got[...].astype(F32)
    new = total[...] + value
    send[...] = new.astype(BF16)
    total_out[...] = new
    upper = (lax.axis_index(AXIS) >> level) & 1
    value = jnp.where(upper == 1, value, 0.0)
    before_out[...] = value if before is None else before[...] + value


def after_last(before, got, ext, send, mine, *, level):
    upper = (lax.axis_index(AXIS) >> level) & 1
    value = jnp.where(upper == 1, got[...].astype(F32), 0.0)
    if before is not None:
        value = before[...] + value
    both = value + ext[...]
    first = side_bit() == 0
    send[...] = jnp.where(first, both, value).astype(BF16)
    mine[...] = jnp.where(first, value, both)


def after_base(mine, got, ext, send, prior):
    rows = mine.shape[0]
    side, first = side_bit(), core_bit() == 0
    for which, value in ((side, mine[...]), (1 - side, got[...].astype(F32))):
        here = pl.ds(aligned(which, rows), rows)
        both = value + ext[here, :]
        send[here, :] = jnp.where(first, both, value).astype(BF16)
        prior[here, :] = jnp.where(first, value, both).astype(BF16)


def intra_kernel(q_ref, k_ref, v_ref, out, intra_ref, sems, *, start):
    count, width = intra_ref.shape
    mid = count // 2
    first = first_lanes((count, PAIR))
    rows = lax.broadcasted_iota(jnp.int32, (mid, mid), 0)
    cols = lax.broadcasted_iota(jnp.int32, (mid, mid), 1)
    causal = cols <= rows
    copies = []
    for p in range(width // PAIR):
        lanes = pl.ds(p * PAIR, PAIR)
        there = pl.ds(start + p * PAIR, PAIR)
        fq = jnp.maximum(q_ref[:, there], 0)
        fk = jnp.maximum(k_ref[:, there], 0)
        val = v_ref[:, there]
        zero = jnp.zeros_like(fq)
        top, low, weights = [], [], []
        for h in range(2):
            mine = first if h == 0 else jnp.logical_not(first)
            mine_q = jnp.where(mine, fq, zero)
            s_top = dot(mine_q[:mid], fk[:mid], ((1,), (1,)))
            s_low = dot(mine_q[mid:], fk, ((1,), (1,)))
            s_top = jnp.where(causal, s_top, 0.0).astype(BF16)
            s_diag = jnp.where(causal, s_low[:, mid:], 0.0).astype(BF16)
            s_low = jnp.concatenate([s_low[:, :mid].astype(BF16), s_diag], axis=1)
            top.append(s_top)
            low.append(s_low)
            weights.append(jnp.where(mine, val, zero))
        w_top = jnp.concatenate([w[:mid] for w in weights], axis=0)
        intra_ref[:mid, lanes] = dot(jnp.concatenate(top, axis=1), w_top, ((1,), (0,)))
        w_low = jnp.concatenate(weights, axis=0)
        intra_ref[mid:, lanes] = dot(jnp.concatenate(low, axis=1), w_low, ((1,), (0,)))
        copies.append(pltpu.make_async_copy(intra_ref.at[:, lanes], out.at[:, lanes], sems.at[p]))
        copies[-1].start()
    for copy in copies:
        copy.wait()


def final_kernel(prior_ref, q_ref, in0, in1, gain_ref, *rest, step):
    out_hbm, in_buf, out_buf, in_sems, sems = rest[-5:]
    half = out_buf.shape[1]
    width = half // 2
    core = core_bit()
    base = aligned(core if step == 0 else 1 - core, half)
    loads = []
    for n, src in enumerate((in0, in1)):
        loads.append(pltpu.make_async_copy(src, in_buf.at[:, pl.ds(n * width, width)], in_sems.at[n]))
        loads[-1].start()
    lane = lax.broadcasted_iota(jnp.int32, (QUAD, QUAD), 1) // HEAD_DIM
    row = lax.broadcasted_iota(jnp.int32, (QUAD, QUAD), 0) // HEAD_DIM
    same = lane == row
    ones = jnp.where(same, 1.0 / HEAD_DIM, 0.0).astype(BF16)
    copies = []
    for quad in range(half // QUAD):
        lanes = pl.ds(quad * QUAD, QUAD)
        one = prior_ref[pl.ds(quad * PAIR, HEAD_DIM), :]
        two = prior_ref[pl.ds(quad * PAIR + HEAD_DIM, HEAD_DIM), :]
        wide = jnp.concatenate([one, two], axis=1)
        block = jnp.concatenate([wide] * 4, axis=0)
        block = jnp.where(same, block, jnp.zeros_like(block))
        q_lanes = pl.ds((0 if step == 1 else half) + quad * QUAD, QUAD)
        fq = jnp.maximum(q_ref[:, q_lanes], 0)
        if quad * QUAD % width == 0:
            loads[quad * QUAD // width].wait()
        numer = dot(fq, block, ((1,), (0,))) + in_buf[:, lanes]
        square = (numer * numer).astype(BF16)
        mean_sq = dot(square, ones, ((1,), (0,)))
        there = pl.ds(pl.multiple_of(base + quad * QUAD, QUAD), QUAD)
        normed = numer * lax.rsqrt(mean_sq + EPS) * gain_ref[:, there]
        out_buf[:, lanes] = normed.astype(BF16)
        copies.append(pltpu.make_async_copy(out_buf.at[:, lanes], out_hbm.at[:, there], sems.at[quad]))
        copies[-1].start()
    for copy in copies:
        copy.wait()


ANY = pl.BlockSpec(memory_space=pl.ANY)
HBM = pl.BlockSpec(memory_space=pltpu.HBM)
VMEM = pl.BlockSpec(memory_space=pltpu.VMEM)
DMA = pltpu.SemaphoreType.DMA


def call(kernel, outs, args, specs=None, out_specs=None, scratch=(), alias=None, cost=(10_000, 10_000)):
    specs = [VMEM] * len(args) if specs is None else specs
    args = [a if s is ANY else pltpu.with_memory_space_constraint(a, s.memory_space) for a, s in zip(args, specs)]
    many = isinstance(outs, (tuple, list))
    return pl.pallas_call(
        kernel,
        out_shape=outs,
        in_specs=specs,
        out_specs=([VMEM] * len(outs) if many else VMEM) if out_specs is None else out_specs,
        scratch_shapes=scratch,
        input_output_aliases=alias or {},
        compiler_params=pltpu.CompilerParams(vmem_limit_bytes=12 * 2**20),
        cost_estimate=pl.CostEstimate(flops=cost[0], transcendentals=0, bytes_accessed=cost[1]),
    )(*args)


def on_device(queries, keys, values, gain, *, size):
    count, width = queries.shape
    half, part = width // 2, width // 4
    rows = half // PAIR * HEAD_DIM
    quarter = rows // 2
    wide = pltpu.VMEM((count, width), BF16)

    def swap(x, level):
        return lax.ppermute(x, AXIS, [(i, i ^ (1 << level)) for i in range(size)])

    def small(dtype, n=quarter):
        return pltpu.VMEM((n, PAIR), dtype)

    send, k_vmem, v_vmem = call(
        send_kernel,
        (small(BF16, rows), wide, wide),
        (keys, values),
        specs=[HBM, HBM],
        scratch=[DMA((2, 2))],
        cost=(150_000_000, 2_000_000),
    )
    got = swap(send, 0)
    keep, q_vmem = call(
        keep_kernel,
        (small(F32, rows), wide),
        (k_vmem, v_vmem, queries),
        specs=[VMEM, VMEM, HBM],
        scratch=[DMA((2,))],
        cost=(150_000_000, 1_000_000),
    )
    parts = [
        call(
            functools.partial(intra_kernel, start=n * part),
            jax.ShapeDtypeStruct((count, part), F32),
            (q_vmem, k_vmem, v_vmem),
            out_specs=ANY,
            scratch=[pltpu.VMEM((count, part), F32), DMA((part // PAIR,))],
            cost=(150_000_000, 1_500_000),
        )
        for n in range(4)
    ]
    send, own, ext_core = call(after_core, (small(BF16), small(F32), small(F32, rows)), (keep, got))
    got = swap(send, 1)
    send, total, ext_side = call(after_side, (small(BF16), small(F32), small(F32)), (own, got))
    before = None
    level = 2
    while 1 << level < size:
        got = swap(send, level)
        last = 1 << (level + 1) >= size
        kernel = functools.partial(after_last if last else after_outer, level=level)
        args = [got, ext_side] if last else [got]
        if before is None:
            kernel = functools.partial(lambda k, *a: k(a[0], None, *a[1:]), kernel) if not last else functools.partial(lambda k, *a: k(None, *a), kernel)
        else:
            args = [before, *args]
        if last:
            send, mine = call(kernel, (small(BF16), small(F32)), args)
        else:
            send, total, before = call(kernel, (small(BF16), small(F32), small(F32)), [total, *args])
        level += 1
    got = swap(send, 1)
    send, prior = call(after_base, (small(BF16, rows), small(BF16, rows)), (mine, got, ext_core))
    got = swap(send, 0)

    out = None
    for step, prior in ((0, prior), (1, got)):
        args = [prior, q_vmem, *(parts[2:] if step == 0 else parts[:2]), gain[None, :]]
        specs = [VMEM, VMEM, ANY, ANY, VMEM]
        if out is not None:
            args.append(out)
            specs.append(ANY)
        out = call(
            functools.partial(final_kernel, step=step),
            jax.ShapeDtypeStruct((count, width), BF16),
            args,
            specs=specs,
            out_specs=ANY,
            scratch=[
                pltpu.VMEM((count, half), F32),
                pltpu.VMEM((count, half), BF16),
                DMA((2,)),
                DMA((half // QUAD,)),
            ],
            alias={} if out is None else {5: 0},
            cost=(100_000_000, 2_000_000),
        )
    return out


def solution(mesh):
    return jax.shard_map(
        functools.partial(on_device, size=mesh.shape[AXIS]),
        mesh=mesh,
        in_specs=(
            P(("groups", "seq"), None),
            P(("groups", "seq"), None),
            P(("groups", "seq"), None),
            P(),
        ),
        out_specs=P(("groups", "seq"), None),
        check_vma=False,
    )
```

```python
import functools

import jax
import jax.numpy as jnp
from jax import lax
from jax.experimental import pallas as pl
from jax.experimental.pallas import tpu as pltpu
from jax.sharding import PartitionSpec as P


HEAD_DIM = 64
PAIR = 2 * HEAD_DIM
QUAD = 4 * HEAD_DIM
EPS = 1e-05
AXIS = "seq"
BF16, F32 = jnp.bfloat16, jnp.float32


def core_bit():
    return lax.axis_index(AXIS) & 1


def side_bit():
    return (lax.axis_index(AXIS) >> 1) & 1


def aligned(index, by):
    return pl.multiple_of(index * by, by)


def first_lanes(shape):
    return lax.broadcasted_iota(jnp.int32, shape, len(shape) - 1) % PAIR < HEAD_DIM


def dot(a, b, dims):
    return lax.dot_general(a, b, (dims, ((), ())), preferred_element_type=F32)


def slot_start(slot, part):
    core, side = core_bit(), side_bit()
    quarter = 2 * (core if slot >= 2 else 1 - core) + (side if slot % 2 else 1 - side)
    return aligned(quarter, part)


def load_slot(src, dst, slot, at, part, sem):
    there, here = pl.ds(slot_start(slot, part), part), pl.ds(at * part, part)
    load = pltpu.make_async_copy(src.at[:, there], dst.at[:, here], sem)
    load.start()
    return load


def states_of(k_ref, v_ref, out_ref, at, part):
    first = first_lanes((HEAD_DIM, PAIR))
    base = at * part // PAIR * HEAD_DIM
    for quad in range(part // QUAD):
        lanes = pl.ds(at * part + quad * QUAD, QUAD)
        fk = jnp.maximum(k_ref[:, lanes], 0)
        full = dot(fk, v_ref[:, lanes], ((0,), (0,)))
        for p in range(2):
            top = p * PAIR
            rows = full[top : top + PAIR, top : top + PAIR]
            packed = jnp.where(first, rows[:HEAD_DIM], rows[HEAD_DIM:])
            out_ref[pl.ds(base + (quad * 2 + p) * HEAD_DIM, HEAD_DIM), :] = packed.astype(out_ref.dtype)


def state_kernel(k_hbm, v_hbm, *rest, slots, extra):
    sources, rest = rest[: len(extra)], rest[len(extra) :]
    state_ref, k_ref, v_ref, *more, sems, more_sems = rest
    part = k_ref.shape[1] // 2
    loads = []
    for at, slot in enumerate(slots):
        for n, (src, dst) in enumerate(((k_hbm, k_ref), (v_hbm, v_ref))):
            loads.append(load_slot(src, dst, slot, at, part, sems.at[at, n]))
    late = []
    for n, (src, dst, kind) in enumerate(zip(sources, more, extra)):
        if kind == "slots":
            for at, slot in enumerate(slots):
                late.append(load_slot(src, dst, slot, at, part, more_sems.at[n, at]))
        else:
            late.append(pltpu.make_async_copy(src, dst, more_sems.at[n, 0]))
            late[-1].start()
    for at in range(2):
        loads[2 * at].wait()
        loads[2 * at + 1].wait()
        states_of(k_ref, v_ref, state_ref, at, part)
    for load in late:
        load.wait()


def after_core(keep, got, send, own, ext):
    rows = own.shape[0]
    state, other = keep[...], got[...].astype(F32)
    both = state + other
    send[...] = both[:rows].astype(BF16)
    own[...] = both[rows:]
    ext[...] = jnp.where(core_bit() == 0, state, other)


def after_side(own, got, send, total, ext):
    value = own[...] + got[...].astype(F32)
    send[...] = value.astype(BF16)
    total[...] = value
    ext[...] = jnp.where(side_bit() == 0, own[...], got[...].astype(F32))


def upper_part(before, got, level):
    upper = (lax.axis_index(AXIS) >> level) & 1
    value = jnp.where(upper == 1, got[...].astype(F32), 0.0)
    return value if before is None else before[...] + value


def after_outer(refs, *, level, start, more):
    refs = list(refs)
    total = refs.pop(0)
    before = None if start else refs.pop(0)
    got, send, before_out, *total_out = refs
    new = total[...] + got[...].astype(F32)
    send[...] = new.astype(BF16)
    before_out[...] = upper_part(before, got, level)
    if more:
        total_out[0][...] = new


def after_last(refs, *, level, start):
    refs = list(refs)
    before = None if start else refs.pop(0)
    got, ext_side, ext_core, send, send_core, prior = refs
    value = upper_part(before, got, level)
    both = value + ext_side[...]
    first = side_bit() == 0
    send[...] = jnp.where(first, both, value).astype(BF16)
    split_cores(jnp.where(first, value, both), ext_core[value.shape[0] :, :], send_core, prior)


def split_cores(base, ext, send_core, prior):
    both = base + ext
    first = core_bit() == 0
    send_core[...] = jnp.where(first, both, base).astype(BF16)
    prior[...] = jnp.where(first, base, both).astype(BF16)


def after_base(got, ext_core, send_core, prior):
    split_cores(got[...].astype(F32), ext_core[: got.shape[0], :], send_core, prior)


def intra_kernel(refs, *, pairs, load):
    refs = list(refs)
    if load:
        q_hbm, q_hi, k_lo, v_lo, k_hi, v_hi, intra_ref, q_lo, sems = refs
        half = k_hi.shape[1]
        loads = [load_slot(q_hbm, q_lo, slot, slot, half // 2, sems.at[slot]) for slot in (1, 0)]
    else:
        q_lo, q_hi, k_lo, v_lo, k_hi, v_hi, intra_ref = refs
        half = k_hi.shape[1]
        loads = []
    count = intra_ref.shape[0]
    mid = count // 2
    first = first_lanes((count, PAIR))
    rows = lax.broadcasted_iota(jnp.int32, (mid, mid), 0)
    cols = lax.broadcasted_iota(jnp.int32, (mid, mid), 1)
    causal = cols <= rows
    for p in pairs:
        lanes = pl.ds((p - min(pairs)) * PAIR, PAIR)
        high = p * PAIR >= half
        q_ref, k_ref, v_ref = (q_hi, k_hi, v_hi) if high else (q_lo, k_lo, v_lo)
        if loads and not high:
            for copy in loads:
                copy.wait()
            loads = []
        there = pl.ds(p * PAIR % half, PAIR)
        fq = jnp.maximum(q_ref[:, there], 0)
        fk = jnp.maximum(k_ref[:, there], 0)
        val = v_ref[:, there]
        zero = jnp.zeros_like(fq)
        top, low, weights = [], [], []
        for h in range(2):
            mine = first if h == 0 else jnp.logical_not(first)
            mine_q = jnp.where(mine, fq, zero)
            s_top = dot(mine_q[:mid], fk[:mid], ((1,), (1,)))
            s_low = dot(mine_q[mid:], fk, ((1,), (1,)))
            s_top = jnp.where(causal, s_top, 0.0).astype(BF16)
            s_diag = jnp.where(causal, s_low[:, mid:], 0.0).astype(BF16)
            s_low = jnp.concatenate([s_low[:, :mid].astype(BF16), s_diag], axis=1)
            top.append(s_top)
            low.append(s_low)
            weights.append(jnp.where(mine, val, zero))
        w_top = jnp.concatenate([w[:mid] for w in weights], axis=0)
        intra_ref[:mid, lanes] = dot(jnp.concatenate(top, axis=1), w_top, ((1,), (0,)))
        w_low = jnp.concatenate(weights, axis=0)
        intra_ref[mid:, lanes] = dot(jnp.concatenate(low, axis=1), w_low, ((1,), (0,)))
    for copy in loads:
        copy.wait()


def final_kernel(refs, *, slot, places, aliased):
    refs = list(refs)
    prior_ref, q_ref, gain_ref = refs[:3]
    intra_refs = refs[3 : 3 + len(places)]
    out_hbm, out_buf, sems = refs[-3:]
    count, part = out_buf.shape
    base = slot_start(slot, part)
    lane = lax.broadcasted_iota(jnp.int32, (QUAD, QUAD), 1) // HEAD_DIM
    row = lax.broadcasted_iota(jnp.int32, (QUAD, QUAD), 0) // HEAD_DIM
    same = lane == row
    ones = jnp.where(same, 1.0 / HEAD_DIM, 0.0).astype(BF16)
    blocks = 2
    step = count // blocks
    copies = []
    for quad in range(part // QUAD):
        lanes = pl.ds(quad * QUAD, QUAD)
        one = prior_ref[pl.ds(quad * PAIR, HEAD_DIM), :]
        two = prior_ref[pl.ds(quad * PAIR + HEAD_DIM, HEAD_DIM), :]
        wide = jnp.concatenate([one, two], axis=1)
        block = jnp.concatenate([wide] * 4, axis=0)
        block = jnp.where(same, block, jnp.zeros_like(block))
        there = pl.ds(pl.multiple_of(base + quad * QUAD, QUAD), QUAD)
        gain = gain_ref[:, there]
        for n in range(blocks):
            tokens = pl.ds(n * step, step)
            fq = jnp.maximum(q_ref[tokens, pl.ds(slot % 2 * part + quad * QUAD, QUAD)], 0)
            intra = intra_refs[quad][tokens, pl.ds(places[quad], QUAD)]
            numer = dot(fq, block, ((1,), (0,))) + intra
            square = (numer * numer).astype(BF16)
            mean_sq = dot(square, ones, ((1,), (0,)))
            normed = numer * lax.rsqrt(mean_sq + EPS) * gain
            out_buf[tokens, lanes] = normed.astype(BF16)
            copies.append(
                pltpu.make_async_copy(out_buf.at[tokens, lanes], out_hbm.at[tokens, there], sems.at[quad, n])
            )
            copies[-1].start()
    for copy in copies:
        copy.wait()


ANY = pl.BlockSpec(memory_space=pl.ANY)
HBM = pl.BlockSpec(memory_space=pltpu.HBM)
VMEM = pl.BlockSpec(memory_space=pltpu.VMEM)
DMA = pltpu.SemaphoreType.DMA


def call(kernel, outs, args, specs=None, out_specs=None, scratch=(), alias=None, cost=(10_000, 10_000)):
    specs = [VMEM] * len(args) if specs is None else specs
    args = [a if s is ANY else pltpu.with_memory_space_constraint(a, s.memory_space) for a, s in zip(args, specs)]
    many = isinstance(outs, (tuple, list))
    return pl.pallas_call(
        kernel,
        out_shape=outs,
        in_specs=specs,
        out_specs=([VMEM] * len(outs) if many else VMEM) if out_specs is None else out_specs,
        scratch_shapes=scratch,
        input_output_aliases=alias or {},
        compiler_params=pltpu.CompilerParams(vmem_limit_bytes=12 * 2**20),
        cost_estimate=pl.CostEstimate(flops=cost[0], transcendentals=0, bytes_accessed=cost[1]),
    )(*args)


def packed(kernel, **static):
    return lambda *refs: kernel(refs, **static)


def on_device(queries, keys, values, gain, *, size):
    count, width = queries.shape
    half, part = width // 2, width // 4
    rows = half // PAIR * HEAD_DIM
    quarter = rows // 2
    columns = pltpu.VMEM((count, half), BF16)

    def swap(x, level):
        return lax.ppermute(x, AXIS, [(i, i ^ (1 << level)) for i in range(size)])

    def small(dtype, n=quarter):
        return pltpu.VMEM((n, PAIR), dtype)

    send, k_lo, v_lo = call(
        functools.partial(state_kernel, slots=(0, 1), extra=()),
        (small(BF16, rows), columns, columns),
        (keys, values),
        specs=[HBM] * 2,
        scratch=[DMA((2, 2)), DMA((1, 1))],
        cost=(150_000_000, 2_000_000),
    )
    got = swap(send, 0)
    keep, k_hi, v_hi, q_hi, gain_vmem = call(
        functools.partial(state_kernel, slots=(2, 3), extra=("slots", "whole")),
        (small(F32, rows), columns, columns, columns, pltpu.VMEM((1, width), F32)),
        (keys, values, queries, gain[None, :]),
        specs=[HBM] * 4,
        scratch=[DMA((2, 2)), DMA((2, 2))],
        cost=(150_000_000, 2_000_000),
    )
    pairs = width // PAIR
    cuts = (pairs // 2 + pairs // 8, pairs // 2 - pairs // 4, 0)
    groups = ((cuts[0], pairs), (cuts[1], cuts[0]), (cuts[2], cuts[1]))
    tiles = (k_lo, v_lo, k_hi, v_hi)
    q_lo, parts = queries, []
    for n, (low, high) in enumerate(groups):
        load = n == 1
        order = tuple(range(low, high)) if n != 1 else tuple(range(high - 1, low - 1, -1))
        buffer = pltpu.VMEM((count, (high - low) * PAIR), F32)
        outs = call(
            packed(intra_kernel, pairs=order, load=load) if n else packed(lambda r, **kw: intra_kernel((None, *r), **kw), pairs=order, load=False),
            (buffer, columns) if load else buffer,
            (q_lo, q_hi, *tiles) if n else (q_hi, *tiles),
            specs=[HBM] + [VMEM] * 5 if load else None,
            scratch=[DMA((2,))] if load else (),
            cost=(200_000_000, 1_500_000),
        )
        if load:
            outs, q_lo = outs
        parts.append(outs)

    send, own, ext_core = call(after_core, (small(BF16), small(F32), small(F32, rows)), (keep, got))
    got = swap(send, 1)
    send, total, ext_side = call(after_side, (small(BF16), small(F32), small(F32)), (own, got))
    before = []
    level = 2
    while 1 << level < size:
        got = swap(send, level)
        if 1 << (level + 1) < size:
            more = 1 << (level + 2) < size
            send, *before = call(
                packed(after_outer, level=level, start=not before, more=more),
                (small(BF16), *[small(F32)] * (1 + more)),
                [total, *before, got],
            )
            if more:
                total = before.pop()
        else:
            send, send_core, prior3 = call(
                packed(after_last, level=level, start=not before),
                (small(BF16), small(BF16), small(BF16)),
                [*before, got, ext_side, ext_core],
            )
        level += 1
    got = swap(send, 1)
    prior1 = swap(send_core, 0)
    send_core, prior2 = call(after_base, (small(BF16), small(BF16)), (got, ext_core))
    prior0 = swap(send_core, 0)

    out = None
    for slot, prior in ((3, prior3), (1, prior1), (2, prior2), (0, prior0)):
        used, places = [], []
        for quad in range(part // QUAD):
            pair = (slot * part + quad * QUAD) // PAIR
            n = next(i for i, (low, high) in enumerate(groups) if low <= pair < high)
            used.append(parts[n])
            places.append((pair - groups[n][0]) * PAIR)
        args = [prior, q_hi if slot >= 2 else q_lo, gain_vmem, *used]
        specs = [VMEM] * len(args)
        if out is not None:
            args.append(out)
            specs.append(ANY)
        out = call(
            packed(final_kernel, slot=slot, places=tuple(places), aliased=out is not None),
            jax.ShapeDtypeStruct((count, width), BF16),
            args,
            specs=specs,
            out_specs=ANY,
            scratch=[pltpu.VMEM((count, part), BF16), DMA((part // QUAD, 2))],
            alias={} if out is None else {len(args) - 1: 0},
            cost=(50_000_000, 1_000_000),
        )
    return out


def solution(mesh):
    return jax.shard_map(
        functools.partial(on_device, size=mesh.shape[AXIS]),
        mesh=mesh,
        in_specs=(
            P(("groups", "seq"), None),
            P(("groups", "seq"), None),
            P(("groups", "seq"), None),
            P(),
        ),
        out_specs=P(("groups", "seq"), None),
        check_vma=False,
    )
```

```python
import functools

import jax
import jax.numpy as jnp
from jax import lax
from jax.experimental import pallas as pl
from jax.experimental.pallas import tpu as pltpu
from jax.sharding import PartitionSpec as P


HEAD_DIM = 64
PAIR = 2 * HEAD_DIM
QUAD = 4 * HEAD_DIM
EPS = 1e-05
AXIS = "seq"
BF16, F32 = jnp.bfloat16, jnp.float32


def core_bit():
    return lax.axis_index(AXIS) & 1


def side_bit():
    return (lax.axis_index(AXIS) >> 1) & 1


def aligned(index, by):
    return pl.multiple_of(index * by, by)


def first_lanes(shape):
    return lax.broadcasted_iota(jnp.int32, shape, len(shape) - 1) % PAIR < HEAD_DIM


def dot(a, b, dims):
    return lax.dot_general(a, b, (dims, ((), ())), preferred_element_type=F32)


def slot_start(slot, part):
    core, side = core_bit(), side_bit()
    quarter = 2 * (core if slot >= 2 else 1 - core) + (side if slot % 2 else 1 - side)
    return aligned(quarter, part)


def load_slot(src, dst, slot, at, part, sem):
    there, here = pl.ds(slot_start(slot, part), part), pl.ds(at * part, part)
    load = pltpu.make_async_copy(src.at[:, there], dst.at[:, here], sem)
    load.start()
    return load


def states_of(k_ref, v_ref, out_ref, at, part):
    first = first_lanes((HEAD_DIM, PAIR))
    base = at * part // PAIR * HEAD_DIM
    for quad in range(part // QUAD):
        lanes = pl.ds(at * part + quad * QUAD, QUAD)
        fk = jnp.maximum(k_ref[:, lanes], 0)
        full = dot(fk, v_ref[:, lanes], ((0,), (0,)))
        for p in range(2):
            top = p * PAIR
            rows = full[top : top + PAIR, top : top + PAIR]
            packed = jnp.where(first, rows[:HEAD_DIM], rows[HEAD_DIM:])
            out_ref[pl.ds(base + (quad * 2 + p) * HEAD_DIM, HEAD_DIM), :] = packed.astype(out_ref.dtype)


def send_kernel(k_hbm, v_hbm, send_ref, k_lo, v_lo, k_hi, v_hi, sems):
    part = k_lo.shape[1] // 2
    loads = []
    for slot in range(4):
        for n, (src, dst) in enumerate(((k_hbm, k_lo if slot < 2 else k_hi), (v_hbm, v_lo if slot < 2 else v_hi))):
            loads.append(load_slot(src, dst, slot, slot % 2, part, sems.at[slot, n]))
    for slot in range(2):
        loads[2 * slot].wait()
        loads[2 * slot + 1].wait()
        states_of(k_lo, v_lo, send_ref, slot, part)
    for load in loads[4:]:
        load.wait()


def keep_kernel(k_ref, v_ref, q_hbm, gain_hbm, keep_ref, q_ref, gain_ref, sems):
    part = k_ref.shape[1] // 2
    loads = [load_slot(q_hbm, q_ref, 2 + at, at, part, sems.at[at]) for at in range(2)]
    loads.append(pltpu.make_async_copy(gain_hbm, gain_ref, sems.at[2]))
    loads[-1].start()
    for at in range(2):
        states_of(k_ref, v_ref, keep_ref, at, part)
    for load in loads:
        load.wait()


def after_core(keep, got, send, own, ext):
    rows = own.shape[0]
    state, other = keep[...], got[...].astype(F32)
    both = state + other
    send[...] = both[:rows].astype(BF16)
    own[...] = both[rows:]
    ext[...] = jnp.where(core_bit() == 0, state, other)


def after_side(own, got, send, total, ext):
    value = own[...] + got[...].astype(F32)
    send[...] = value.astype(BF16)
    total[...] = value
    ext[...] = jnp.where(side_bit() == 0, own[...], got[...].astype(F32))


def upper_part(before, got, level):
    upper = (lax.axis_index(AXIS) >> level) & 1
    value = jnp.where(upper == 1, got[...].astype(F32), 0.0)
    return value if before is None else before[...] + value


def after_outer(refs, *, level, start, more):
    refs = list(refs)
    total = refs.pop(0)
    before = None if start else refs.pop(0)
    got, send, before_out, *total_out = refs
    new = total[...] + got[...].astype(F32)
    send[...] = new.astype(BF16)
    before_out[...] = upper_part(before, got, level)
    if more:
        total_out[0][...] = new


def after_last(refs, *, level, start):
    refs = list(refs)
    before = None if start else refs.pop(0)
    got, ext_side, ext_core, send, send_core, prior = refs
    value = upper_part(before, got, level)
    both = value + ext_side[...]
    first = side_bit() == 0
    send[...] = jnp.where(first, both, value).astype(BF16)
    split_cores(jnp.where(first, value, both), ext_core[value.shape[0] :, :], send_core, prior)


def split_cores(base, ext, send_core, prior):
    both = base + ext
    first = core_bit() == 0
    send_core[...] = jnp.where(first, both, base).astype(BF16)
    prior[...] = jnp.where(first, base, both).astype(BF16)


def after_base(got, ext_core, send_core, prior):
    split_cores(got[...].astype(F32), ext_core[: got.shape[0], :], send_core, prior)


def intra_kernel(refs, *, pairs, load):
    refs = list(refs)
    if load:
        q_hbm, q_hi, k_lo, v_lo, k_hi, v_hi, intra_ref, q_lo, sems = refs
        half = k_hi.shape[1]
        loads = [load_slot(q_hbm, q_lo, slot, slot, half // 2, sems.at[slot]) for slot in (1, 0)]
    else:
        q_lo, q_hi, k_lo, v_lo, k_hi, v_hi, intra_ref = refs
        half = k_hi.shape[1]
        loads = []
    count = intra_ref.shape[0]
    mid = count // 2
    first = first_lanes((count, PAIR))
    rows = lax.broadcasted_iota(jnp.int32, (mid, mid), 0)
    cols = lax.broadcasted_iota(jnp.int32, (mid, mid), 1)
    causal = cols <= rows
    for p in pairs:
        lanes = pl.ds((p - min(pairs)) * PAIR, PAIR)
        high = p * PAIR >= half
        q_ref, k_ref, v_ref = (q_hi, k_hi, v_hi) if high else (q_lo, k_lo, v_lo)
        if loads and not high:
            for copy in loads:
                copy.wait()
            loads = []
        there = pl.ds(p * PAIR % half, PAIR)
        fq = jnp.maximum(q_ref[:, there], 0)
        fk = jnp.maximum(k_ref[:, there], 0)
        val = v_ref[:, there]
        zero = jnp.zeros_like(fq)
        top, low, weights = [], [], []
        for h in range(2):
            mine = first if h == 0 else jnp.logical_not(first)
            mine_q = jnp.where(mine, fq, zero)
            s_top = dot(mine_q[:mid], fk[:mid], ((1,), (1,)))
            s_low = dot(mine_q[mid:], fk, ((1,), (1,)))
            s_top = jnp.where(causal, s_top, 0.0).astype(BF16)
            s_diag = jnp.where(causal, s_low[:, mid:], 0.0).astype(BF16)
            s_low = jnp.concatenate([s_low[:, :mid].astype(BF16), s_diag], axis=1)
            top.append(s_top)
            low.append(s_low)
            weights.append(jnp.where(mine, val, zero))
        w_top = jnp.concatenate([w[:mid] for w in weights], axis=0)
        intra_ref[:mid, lanes] = dot(jnp.concatenate(top, axis=1), w_top, ((1,), (0,)))
        w_low = jnp.concatenate(weights, axis=0)
        intra_ref[mid:, lanes] = dot(jnp.concatenate(low, axis=1), w_low, ((1,), (0,)))
    for copy in loads:
        copy.wait()


def final_kernel(refs, *, slot, places, aliased):
    refs = list(refs)
    prior_ref, q_ref, gain_ref = refs[:3]
    intra_refs = refs[3 : 3 + len(places)]
    out_hbm, out_buf, sems = refs[-3:]
    count, part = out_buf.shape
    base = slot_start(slot, part)
    lane = lax.broadcasted_iota(jnp.int32, (QUAD, QUAD), 1) // HEAD_DIM
    row = lax.broadcasted_iota(jnp.int32, (QUAD, QUAD), 0) // HEAD_DIM
    same = lane == row
    ones = jnp.where(same, 1.0 / HEAD_DIM, 0.0).astype(BF16)
    blocks = 2
    step = count // blocks
    copies = []
    for quad in range(part // QUAD):
        lanes = pl.ds(quad * QUAD, QUAD)
        one = prior_ref[pl.ds(quad * PAIR, HEAD_DIM), :]
        two = prior_ref[pl.ds(quad * PAIR + HEAD_DIM, HEAD_DIM), :]
        wide = jnp.concatenate([one, two], axis=1)
        block = jnp.concatenate([wide] * 4, axis=0)
        block = jnp.where(same, block, jnp.zeros_like(block))
        there = pl.ds(pl.multiple_of(base + quad * QUAD, QUAD), QUAD)
        gain = gain_ref[:, there]
        for n in range(blocks):
            tokens = pl.ds(n * step, step)
            fq = jnp.maximum(q_ref[tokens, pl.ds(slot % 2 * part + quad * QUAD, QUAD)], 0)
            intra = intra_refs[quad][tokens, pl.ds(places[quad], QUAD)]
            numer = dot(fq, block, ((1,), (0,))) + intra
            square = (numer * numer).astype(BF16)
            mean_sq = dot(square, ones, ((1,), (0,)))
            normed = numer * lax.rsqrt(mean_sq + EPS) * gain
            out_buf[tokens, lanes] = normed.astype(BF16)
            copies.append(
                pltpu.make_async_copy(out_buf.at[tokens, lanes], out_hbm.at[tokens, there], sems.at[quad, n])
            )
            copies[-1].start()
    for copy in copies:
        copy.wait()


ANY = pl.BlockSpec(memory_space=pl.ANY)
HBM = pl.BlockSpec(memory_space=pltpu.HBM)
VMEM = pl.BlockSpec(memory_space=pltpu.VMEM)
DMA = pltpu.SemaphoreType.DMA


def call(kernel, outs, args, specs=None, out_specs=None, scratch=(), alias=None, cost=(10_000, 10_000)):
    specs = [VMEM] * len(args) if specs is None else specs
    args = [a if s is ANY else pltpu.with_memory_space_constraint(a, s.memory_space) for a, s in zip(args, specs)]
    many = isinstance(outs, (tuple, list))
    return pl.pallas_call(
        kernel,
        out_shape=outs,
        in_specs=specs,
        out_specs=([VMEM] * len(outs) if many else VMEM) if out_specs is None else out_specs,
        scratch_shapes=scratch,
        input_output_aliases=alias or {},
        compiler_params=pltpu.CompilerParams(vmem_limit_bytes=12 * 2**20),
        cost_estimate=pl.CostEstimate(flops=cost[0], transcendentals=0, bytes_accessed=cost[1]),
    )(*args)


def packed(kernel, **static):
    return lambda *refs: kernel(refs, **static)


def on_device(queries, keys, values, gain, *, size):
    count, width = queries.shape
    half, part = width // 2, width // 4
    rows = half // PAIR * HEAD_DIM
    quarter = rows // 2
    columns = pltpu.VMEM((count, half), BF16)

    def swap(x, level):
        return lax.ppermute(x, AXIS, [(i, i ^ (1 << level)) for i in range(size)])

    def small(dtype, n=quarter):
        return pltpu.VMEM((n, PAIR), dtype)

    send, *tiles = call(
        send_kernel,
        (small(BF16, rows), *[columns] * 4),
        (keys, values),
        specs=[HBM] * 2,
        scratch=[DMA((4, 2))],
        cost=(150_000_000, 2_000_000),
    )
    got = swap(send, 0)
    keep, q_hi, gain_vmem = call(
        keep_kernel,
        (small(F32, rows), columns, pltpu.VMEM((1, width), F32)),
        (*tiles[2:], queries, gain[None, :]),
        specs=[VMEM] * 2 + [HBM] * 2,
        scratch=[DMA((3,))],
        cost=(150_000_000, 2_000_000),
    )
    pairs = width // PAIR
    cuts = (pairs // 2 + pairs // 8, pairs // 2 - pairs // 4, 0)
    groups = ((cuts[0], pairs), (cuts[1], cuts[0]), (cuts[2], cuts[1]))
    q_lo, parts = queries, []
    for n, (low, high) in enumerate(groups):
        load = n == 1
        order = tuple(range(low, high)) if n != 1 else tuple(range(high - 1, low - 1, -1))
        buffer = pltpu.VMEM((count, (high - low) * PAIR), F32)
        outs = call(
            packed(intra_kernel, pairs=order, load=load) if n else packed(lambda r, **kw: intra_kernel((None, *r), **kw), pairs=order, load=False),
            (buffer, columns) if load else buffer,
            (q_lo, q_hi, *tiles) if n else (q_hi, *tiles),
            specs=[HBM] + [VMEM] * 5 if load else None,
            scratch=[DMA((2,))] if load else (),
            cost=(200_000_000, 1_500_000),
        )
        if load:
            outs, q_lo = outs
        parts.append(outs)

    send, own, ext_core = call(after_core, (small(BF16), small(F32), small(F32, rows)), (keep, got))
    got = swap(send, 1)
    send, total, ext_side = call(after_side, (small(BF16), small(F32), small(F32)), (own, got))
    before = []
    level = 2
    while 1 << level < size:
        got = swap(send, level)
        if 1 << (level + 1) < size:
            more = 1 << (level + 2) < size
            send, *before = call(
                packed(after_outer, level=level, start=not before, more=more),
                (small(BF16), *[small(F32)] * (1 + more)),
                [total, *before, got],
            )
            if more:
                total = before.pop()
        else:
            send, send_core, prior3 = call(
                packed(after_last, level=level, start=not before),
                (small(BF16), small(BF16), small(BF16)),
                [*before, got, ext_side, ext_core],
            )
        level += 1
    got = swap(send, 1)
    prior1 = swap(send_core, 0)
    send_core, prior2 = call(after_base, (small(BF16), small(BF16)), (got, ext_core))
    prior0 = swap(send_core, 0)

    out = None
    for slot, prior in ((3, prior3), (1, prior1), (2, prior2), (0, prior0)):
        used, places = [], []
        for quad in range(part // QUAD):
            pair = (slot * part + quad * QUAD) // PAIR
            n = next(i for i, (low, high) in enumerate(groups) if low <= pair < high)
            used.append(parts[n])
            places.append((pair - groups[n][0]) * PAIR)
        args = [prior, q_hi if slot >= 2 else q_lo, gain_vmem, *used]
        specs = [VMEM] * len(args)
        if out is not None:
            args.append(out)
            specs.append(ANY)
        out = call(
            packed(final_kernel, slot=slot, places=tuple(places), aliased=out is not None),
            jax.ShapeDtypeStruct((count, width), BF16),
            args,
            specs=specs,
            out_specs=ANY,
            scratch=[pltpu.VMEM((count, part), BF16), DMA((part // QUAD, 2))],
            alias={} if out is None else {len(args) - 1: 0},
            cost=(50_000_000, 1_000_000),
        )
    return out


def solution(mesh):
    return jax.shard_map(
        functools.partial(on_device, size=mesh.shape[AXIS]),
        mesh=mesh,
        in_specs=(
            P(("groups", "seq"), None),
            P(("groups", "seq"), None),
            P(("groups", "seq"), None),
            P(),
        ),
        out_specs=P(("groups", "seq"), None),
        check_vma=False,
    )
```

```python
import functools

import jax
import jax.numpy as jnp
from jax import lax
from jax.experimental import pallas as pl
from jax.experimental.pallas import tpu as pltpu
from jax.sharding import PartitionSpec as P


HEAD_DIM = 64
PAIR = 2 * HEAD_DIM
QUAD = 4 * HEAD_DIM
EPS = 1e-05
AXIS = "seq"
BF16, F32 = jnp.bfloat16, jnp.float32


def core_bit():
    return lax.axis_index(AXIS) & 1


def side_bit():
    return (lax.axis_index(AXIS) >> 1) & 1


def aligned(index, by):
    return pl.multiple_of(index * by, by)


def first_lanes(shape):
    return lax.broadcasted_iota(jnp.int32, shape, len(shape) - 1) % PAIR < HEAD_DIM


def dot(a, b, dims):
    return lax.dot_general(a, b, (dims, ((), ())), preferred_element_type=F32)


def slot_start(slot, part):
    core, side = core_bit(), side_bit()
    quarter = 2 * (core if slot >= 2 else 1 - core) + (side if slot % 2 else 1 - side)
    return aligned(quarter, part)


def load_slot(src, dst, slot, sem):
    part = dst.shape[1]
    load = pltpu.make_async_copy(src.at[:, pl.ds(slot_start(slot, part), part)], dst, sem)
    load.start()
    return load


def wait_all(loads):
    for load in loads:
        load.wait()


def states_of(k_ref, v_ref, out_ref):
    first = first_lanes((HEAD_DIM, PAIR))
    for quad in range(k_ref.shape[1] // QUAD):
        lanes = pl.ds(quad * QUAD, QUAD)
        fk = jnp.maximum(k_ref[:, lanes], 0)
        full = dot(fk, v_ref[:, lanes], ((0,), (0,)))
        for p in range(2):
            top = p * PAIR
            rows = full[top : top + PAIR, top : top + PAIR]
            packed = jnp.where(first, rows[:HEAD_DIM], rows[HEAD_DIM:])
            out_ref[pl.ds((quad * 2 + p) * HEAD_DIM, HEAD_DIM), :] = packed.astype(out_ref.dtype)


def first_kernel(k_hbm, v_hbm, send, k0, v0, k2, v2, sems):
    loads = [
        load_slot(src, dst, slot, sems.at[n])
        for n, (src, dst, slot) in enumerate(((k_hbm, k0, 0), (v_hbm, v0, 0), (k_hbm, k2, 2), (v_hbm, v2, 2)))
    ]
    wait_all(loads[:2])
    states_of(k0, v0, send)
    wait_all(loads[2:])


def second_kernel(k_hbm, v_hbm, k2, v2, keep, k1, v1, k3, v3, sems):
    loads = [
        load_slot(src, dst, slot, sems.at[n])
        for n, (src, dst, slot) in enumerate(((k_hbm, k1, 1), (v_hbm, v1, 1), (k_hbm, k3, 3), (v_hbm, v3, 3)))
    ]
    states_of(k2, v2, keep)
    wait_all(loads)


def third_kernel(k1, v1, send):
    states_of(k1, v1, send)


def fourth_kernel(k3, v3, q_hbm, gain_hbm, keep, q2, q3, gain, sems):
    loads = [load_slot(q_hbm, q3, 3, sems.at[0]), load_slot(q_hbm, q2, 2, sems.at[1])]
    loads.append(pltpu.make_async_copy(gain_hbm, gain, sems.at[2]))
    loads[-1].start()
    states_of(k3, v3, keep)
    wait_all(loads)


def after_core(keep, got, send, ext):
    state, other = keep[...], got[...].astype(F32)
    send[...] = (state + other).astype(BF16)
    ext[...] = jnp.where(core_bit() == 0, state, other)


def after_side(keep, got_core, got, send, total, ext_core, ext_side):
    state, other = keep[...], got_core[...].astype(F32)
    own, from_side = state + other, got[...].astype(F32)
    value = own + from_side
    send[...] = value.astype(BF16)
    total[...] = value
    ext_core[...] = jnp.where(core_bit() == 0, state, other)
    ext_side[...] = jnp.where(side_bit() == 0, own, from_side)


def upper_part(before, got, level):
    upper = (lax.axis_index(AXIS) >> level) & 1
    value = jnp.where(upper == 1, got[...].astype(F32), 0.0)
    return value if before is None else before[...] + value


def after_outer(refs, *, level, start, more):
    refs = list(refs)
    total = refs.pop(0)
    before = None if start else refs.pop(0)
    got, send, before_out, *total_out = refs
    new = total[...] + got[...].astype(F32)
    send[...] = new.astype(BF16)
    before_out[...] = upper_part(before, got, level)
    if more:
        total_out[0][...] = new


def after_last(refs, *, level, start):
    refs = list(refs)
    before = None if start else refs.pop(0)
    got, ext_side, ext_core, send, send_core, prior = refs
    value = upper_part(before, got, level)
    both = value + ext_side[...]
    first = side_bit() == 0
    send[...] = jnp.where(first, both, value).astype(BF16)
    split_cores(jnp.where(first, value, both), ext_core[...], send_core, prior)


def split_cores(base, ext, send_core, prior):
    both = base + ext
    first = core_bit() == 0
    send_core[...] = jnp.where(first, both, base).astype(BF16)
    prior[...] = jnp.where(first, base, both).astype(BF16)


def after_base(got, ext_core, send_core, prior):
    split_cores(got[...].astype(F32), ext_core[...], send_core, prior)


def intra_kernel(refs, *, pairs, slots, fetch):
    refs = list(refs)
    q_hbm = refs.pop(0) if fetch else None
    tiles = {slot: [None, refs.pop(0), refs.pop(0)] for slot in slots}
    for slot in slots:
        if slot not in fetch:
            tiles[slot][0] = refs.pop(0)
    intra_ref = refs.pop(0)
    fetched = {slot: refs.pop(0) for slot in fetch}
    loads = {slot: load_slot(q_hbm, ref, slot, refs[-1].at[n]) for n, (slot, ref) in enumerate(fetched.items())}
    for slot in set(fetch) & set(slots):
        tiles[slot][0] = fetched[slot]
    count = intra_ref.shape[0]
    part = tiles[slots[0]][1].shape[1]
    mid = count // 2
    first = first_lanes((count, PAIR))
    rows = lax.broadcasted_iota(jnp.int32, (mid, mid), 0)
    cols = lax.broadcasted_iota(jnp.int32, (mid, mid), 1)
    causal = cols <= rows
    for p in pairs:
        lanes = pl.ds((p - min(pairs)) * PAIR, PAIR)
        slot = p * PAIR // part
        if slot in loads:
            loads.pop(slot).wait()
        q_ref, k_ref, v_ref = tiles[slot]
        there = pl.ds(p * PAIR % part, PAIR)
        fq = jnp.maximum(q_ref[:, there], 0)
        fk = jnp.maximum(k_ref[:, there], 0)
        val = v_ref[:, there]
        zero = jnp.zeros_like(fq)
        top, low, weights = [], [], []
        for h in range(2):
            mine = first if h == 0 else jnp.logical_not(first)
            mine_q = jnp.where(mine, fq, zero)
            s_top = dot(mine_q[:mid], fk[:mid], ((1,), (1,)))
            s_low = dot(mine_q[mid:], fk, ((1,), (1,)))
            s_top = jnp.where(causal, s_top, 0.0).astype(BF16)
            s_diag = jnp.where(causal, s_low[:, mid:], 0.0).astype(BF16)
            s_low = jnp.concatenate([s_low[:, :mid].astype(BF16), s_diag], axis=1)
            top.append(s_top)
            low.append(s_low)
            weights.append(jnp.where(mine, val, zero))
        w_top = jnp.concatenate([w[:mid] for w in weights], axis=0)
        intra_ref[:mid, lanes] = dot(jnp.concatenate(top, axis=1), w_top, ((1,), (0,)))
        w_low = jnp.concatenate(weights, axis=0)
        intra_ref[mid:, lanes] = dot(jnp.concatenate(low, axis=1), w_low, ((1,), (0,)))
    wait_all(loads.values())


def final_kernel(refs, *, slot, places):
    refs = list(refs)
    prior_ref, q_ref, gain_ref = refs[:3]
    intra_refs = refs[3 : 3 + 1 + max(which for which, _ in places)]
    out_hbm, out_buf, sems = refs[-3:]
    part = out_buf.shape[1]
    base = slot_start(slot, part)
    lane = lax.broadcasted_iota(jnp.int32, (PAIR, PAIR), 1) // HEAD_DIM
    row = lax.broadcasted_iota(jnp.int32, (PAIR, PAIR), 0) // HEAD_DIM
    same = lane == row
    ones = jnp.where(same, 1.0 / HEAD_DIM, 0.0).astype(BF16)
    copies = []
    for p, (which, at) in enumerate(places):
        lanes = pl.ds(p * PAIR, PAIR)
        state = prior_ref[pl.ds(p * HEAD_DIM, HEAD_DIM), :]
        block = jnp.concatenate([state, state], axis=0)
        block = jnp.where(same, block, jnp.zeros_like(block))
        there = pl.ds(pl.multiple_of(base + p * PAIR, PAIR), PAIR)
        fq = jnp.maximum(q_ref[:, lanes], 0)
        numer = dot(fq, block, ((1,), (0,))) + intra_refs[which][:, pl.ds(at, PAIR)]
        mean_sq = dot((numer * numer).astype(BF16), ones, ((1,), (0,)))
        normed = numer * lax.rsqrt(mean_sq + EPS) * gain_ref[:, there]
        out_buf[:, lanes] = normed.astype(BF16)
        copies.append(pltpu.make_async_copy(out_buf.at[:, lanes], out_hbm.at[:, there], sems.at[p]))
        copies[-1].start()
    wait_all(copies)


ANY = pl.BlockSpec(memory_space=pl.ANY)
HBM = pl.BlockSpec(memory_space=pltpu.HBM)
VMEM = pl.BlockSpec(memory_space=pltpu.VMEM)
DMA = pltpu.SemaphoreType.DMA


def call(kernel, outs, args, specs=None, out_specs=None, scratch=(), alias=None, cost=(10_000, 10_000)):
    specs = [VMEM] * len(args) if specs is None else specs
    args = [a if s is ANY else pltpu.with_memory_space_constraint(a, s.memory_space) for a, s in zip(args, specs)]
    many = isinstance(outs, (tuple, list))
    return pl.pallas_call(
        kernel,
        out_shape=outs,
        in_specs=specs,
        out_specs=([VMEM] * len(outs) if many else VMEM) if out_specs is None else out_specs,
        scratch_shapes=scratch,
        input_output_aliases=alias or {},
        compiler_params=pltpu.CompilerParams(vmem_limit_bytes=12 * 2**20),
        cost_estimate=pl.CostEstimate(flops=cost[0], transcendentals=0, bytes_accessed=cost[1]),
    )(*args)


def packed(kernel, **static):
    return lambda *refs: kernel(refs, **static)


def on_device(queries, keys, values, gain, *, size):
    count, width = queries.shape
    part = width // 4
    quarter = part // PAIR * HEAD_DIM
    tile = pltpu.VMEM((count, part), BF16)
    k, v, q = [None] * 4, [None] * 4, [None] * 4

    def swap(x, level):
        return lax.ppermute(x, AXIS, [(i, i ^ (1 << level)) for i in range(size)])

    def small(dtype):
        return pltpu.VMEM((quarter, PAIR), dtype)

    send, k[0], v[0], k[2], v[2] = call(
        first_kernel, (small(BF16), *[tile] * 4), (keys, values), specs=[HBM] * 2, scratch=[DMA((4,))]
    )
    got = swap(send, 0)
    keep, k[1], v[1], k[3], v[3] = call(
        second_kernel,
        (small(F32), *[tile] * 4),
        (keys, values, k[2], v[2]),
        specs=[HBM] * 2 + [VMEM] * 2,
        scratch=[DMA((4,))],
        cost=(80_000_000, 2_000_000),
    )
    send, ext_core2 = call(after_core, (small(BF16), small(F32)), (keep, got))
    got = swap(send, 1)
    send = call(third_kernel, small(BF16), (k[1], v[1]), cost=(80_000_000, 500_000))
    got_core = swap(send, 0)
    keep, q[2], q[3], gain_vmem = call(
        fourth_kernel,
        (small(F32), tile, tile, pltpu.VMEM((1, width), F32)),
        (k[3], v[3], queries, gain[None, :]),
        specs=[VMEM] * 2 + [HBM] * 2,
        scratch=[DMA((3,))],
        cost=(80_000_000, 1_000_000),
    )
    pairs = width // PAIR
    cuts = (pairs, pairs * 3 // 4, pairs * 3 // 8, 0)
    groups = tuple(zip(cuts[1:], cuts[:-1]))
    parts = []
    for n, (low, high) in enumerate(groups):
        order = tuple(range(high - 1, low - 1, -1))
        slots = tuple(sorted({p * PAIR // part for p in order}))
        fetch = (1, 0) if n == 1 else ()
        args = [queries] if fetch else []
        for slot in slots:
            args += [k[slot], v[slot]]
        args += [q[slot] for slot in slots if slot not in fetch]
        buffer = pltpu.VMEM((count, (high - low) * PAIR), F32)
        outs = call(
            packed(intra_kernel, pairs=order, slots=slots, fetch=fetch),
            (buffer, *[tile] * len(fetch)) if fetch else buffer,
            args,
            specs=[HBM] + [VMEM] * (len(args) - 1) if fetch else None,
            scratch=[DMA((len(fetch),))] if fetch else (),
            cost=(200_000_000, 1_500_000),
        )
        if fetch:
            outs, *found = outs
            for slot, value in zip(fetch, found):
                q[slot] = value
        parts.append(outs)

    send, total, ext_core3, ext_side = call(
        after_side, (small(BF16), *[small(F32)] * 3), (keep, got_core, got)
    )
    before = []
    level = 2
    while 1 << level < size:
        got = swap(send, level)
        if 1 << (level + 1) < size:
            more = 1 << (level + 2) < size
            send, *before = call(
                packed(after_outer, level=level, start=not before, more=more),
                (small(BF16), *[small(F32)] * (1 + more)),
                [total, *before, got],
            )
            if more:
                total = before.pop()
        else:
            send, send_core, prior3 = call(
                packed(after_last, level=level, start=not before),
                (small(BF16), small(BF16), small(BF16)),
                [*before, got, ext_side, ext_core3],
            )
        level += 1
    got = swap(send, 1)
    prior1 = swap(send_core, 0)
    send_core, prior2 = call(after_base, (small(BF16), small(BF16)), (got, ext_core2))
    prior0 = swap(send_core, 0)

    out = None
    for slot, prior in ((3, prior3), (1, prior1), (2, prior2), (0, prior0)):
        used, places = [], []
        for pair in range(slot * part // PAIR, (slot + 1) * part // PAIR):
            n = next(i for i, (low, high) in enumerate(groups) if low <= pair < high)
            if n not in used:
                used.append(n)
            places.append((used.index(n), (pair - groups[n][0]) * PAIR))
        args = [prior, q[slot], gain_vmem, *[parts[n] for n in used]]
        specs = [VMEM] * len(args)
        if out is not None:
            args.append(out)
            specs.append(ANY)
        out = call(
            packed(final_kernel, slot=slot, places=tuple(places)),
            jax.ShapeDtypeStruct((count, width), BF16),
            args,
            specs=specs,
            out_specs=ANY,
            scratch=[pltpu.VMEM((count, part), BF16), DMA((part // PAIR,))],
            alias={} if out is None else {len(args) - 1: 0},
            cost=(50_000_000, 1_000_000),
        )
    return out


def solution(mesh):
    return jax.shard_map(
        functools.partial(on_device, size=mesh.shape[AXIS]),
        mesh=mesh,
        in_specs=(
            P(("groups", "seq"), None),
            P(("groups", "seq"), None),
            P(("groups", "seq"), None),
            P(),
        ),
        out_specs=P(("groups", "seq"), None),
        check_vma=False,
    )
```

```python
import functools

import jax
import jax.numpy as jnp
from jax import lax
from jax.experimental import pallas as pl
from jax.experimental.pallas import tpu as pltpu
from jax.sharding import PartitionSpec as P


HEAD_DIM = 64
PAIR = 2 * HEAD_DIM
QUAD = 4 * HEAD_DIM
SHIFT = 6
CORE, SIDE = 1, 2
EPS = 1e-05
AXIS = "seq"
BF16, F32 = jnp.bfloat16, jnp.float32


def core_bit():
    return lax.axis_index(AXIS) & 1


def side_bit():
    return (lax.axis_index(AXIS) >> 1) & 1


def aligned(index, by):
    return pl.multiple_of(index * by, by)


def first_lanes(shape):
    return lax.broadcasted_iota(jnp.int32, shape, len(shape) - 1) < HEAD_DIM


def dot(a, b, dims):
    return lax.dot_general(a, b, (dims, ((), ())), preferred_element_type=F32)


def slot_start(slot, part):
    core, side = core_bit(), side_bit()
    quarter = 2 * (core if slot >= 2 else 1 - core) + (side if slot % 2 else 1 - side)
    return aligned(quarter, part)


def load_slot(src, dst, slot, sem):
    part = dst.shape[1]
    load = pltpu.make_async_copy(src.at[:, pl.ds(slot_start(slot, part), part)], dst, sem)
    load.start()
    return load


def wait_all(loads):
    for load in loads:
        load.wait()


def states_of(k_ref, v_ref, out_ref):
    first = first_lanes((HEAD_DIM, PAIR))
    for quad in range(k_ref.shape[1] // QUAD):
        lanes = pl.ds(quad * QUAD, QUAD)
        fk = jnp.maximum(k_ref[:, lanes], 0)
        full = dot(fk, v_ref[:, lanes], ((0,), (0,)))
        for p in range(2):
            top = p * PAIR
            rows = full[top : top + PAIR, top : top + PAIR]
            packed = jnp.where(first, rows[:HEAD_DIM], rows[HEAD_DIM:])
            out_ref[pl.ds((quad * 2 + p) * HEAD_DIM, HEAD_DIM), :] = packed.astype(out_ref.dtype)


def first_kernel(k_hbm, v_hbm, send, k0, v0, k2, v2, sems):
    loads = [
        load_slot(src, dst, slot, sems.at[n])
        for n, (src, dst, slot) in enumerate(((k_hbm, k0, 0), (v_hbm, v0, 0), (k_hbm, k2, 2), (v_hbm, v2, 2)))
    ]
    wait_all(loads[:2])
    states_of(k0, v0, send)
    wait_all(loads[2:])


def second_kernel(k_hbm, v_hbm, k2, v2, keep, k1, v1, k3, v3, sems):
    loads = [
        load_slot(src, dst, slot, sems.at[n])
        for n, (src, dst, slot) in enumerate(((k_hbm, k1, 1), (v_hbm, v1, 1), (k_hbm, k3, 3), (v_hbm, v3, 3)))
    ]
    states_of(k2, v2, keep)
    wait_all(loads)


def third_kernel(k1, v1, send):
    states_of(k1, v1, send)


def fourth_kernel(k3, v3, q_hbm, gain_hbm, keep, q2, q3, gain, sems):
    loads = [load_slot(q_hbm, q3, 3, sems.at[0]), load_slot(q_hbm, q2, 2, sems.at[1])]
    loads.append(pltpu.make_async_copy(gain_hbm, gain, sems.at[2]))
    loads[-1].start()
    states_of(k3, v3, keep)
    wait_all(loads)


def before_core(value):
    return jnp.where(core_bit() == 1, value[...].astype(F32), 0.0)


def after_core(keep, got, send, mine, ext):
    send[...] = (keep[...] + got[...].astype(F32)).astype(BF16)
    mine[...] = keep[...].astype(BF16)
    ext[...] = before_core(got)


def after_side(keep, got_core, got, send, total, ext_core, ext_side):
    state, other = keep[...], got_core[...].astype(F32)
    own, from_side = state + other, got[...].astype(F32)
    value = own + from_side
    send[...] = value.astype(BF16)
    total[...] = value
    ext_core[...] = jnp.where(core_bit() == 0, state, other)
    ext_side[...] = jnp.where(side_bit() == 0, own, from_side)


def upper_part(before, got, level):
    upper = (lax.axis_index(AXIS) >> level) & 1
    value = jnp.where(upper == 1, got[...].astype(F32), 0.0)
    return value if before is None else before[...] + value


def after_outer(refs, *, level, start, more):
    refs = list(refs)
    total = refs.pop(0)
    before = None if start else refs.pop(0)
    got, send, before_out, *total_out = refs
    new = total[...] + got[...].astype(F32)
    send[...] = new.astype(BF16)
    before_out[...] = upper_part(before, got, level)
    if more:
        total_out[0][...] = new


def after_last(refs, *, level, start):
    refs = list(refs)
    before = None if start else refs.pop(0)
    got, ext_side, ext_core, send, send_core, prior = refs
    value = upper_part(before, got, level)
    both = value + ext_side[...]
    first = side_bit() == 0
    send[...] = jnp.where(first, both, value).astype(BF16)
    base = jnp.where(first, value, both)
    ahead = base + ext_core[...]
    core = core_bit()
    send_core[...] = jnp.where(core == 0, ahead, base).astype(BF16)
    prior[...] = jnp.where(core == 0, base, ahead).astype(BF16)


def intra_kernel(refs, *, pairs, slots, fetch):
    refs = list(refs)
    q_hbm = refs.pop(0) if fetch else None
    tiles = {slot: [None, refs.pop(0), refs.pop(0)] for slot in slots}
    for slot in slots:
        if slot not in fetch:
            tiles[slot][0] = refs.pop(0)
    intra_ref = refs.pop(0)
    fetched = {slot: refs.pop(0) for slot in fetch}
    loads = {slot: load_slot(q_hbm, ref, slot, refs[-1].at[n]) for n, (slot, ref) in enumerate(fetched.items())}
    for slot in set(fetch) & set(slots):
        tiles[slot][0] = fetched[slot]
    count = intra_ref.shape[0]
    part = tiles[slots[0]][1].shape[1]
    mid = count // 2
    first = first_lanes((count, PAIR))
    rows = lax.broadcasted_iota(jnp.int32, (mid, mid), 0)
    cols = lax.broadcasted_iota(jnp.int32, (mid, mid), 1)
    causal = cols <= rows
    for p in pairs:
        lanes = pl.ds((p - min(pairs)) * PAIR, PAIR)
        slot = p * PAIR // part
        if slot in loads:
            loads.pop(slot).wait()
        q_ref, k_ref, v_ref = tiles[slot]
        there = pl.ds(p * PAIR % part, PAIR)
        fq = jnp.maximum(q_ref[:, there], 0)
        fk = jnp.maximum(k_ref[:, there], 0)
        val = v_ref[:, there]
        zero = jnp.zeros_like(fq)
        top, low, weights = [], [], []
        for h in range(2):
            mine = first if h == 0 else jnp.logical_not(first)
            mine_q = jnp.where(mine, fq, zero)
            s_top = dot(mine_q[:mid], fk[:mid], ((1,), (1,)))
            s_low = dot(mine_q[mid:], fk, ((1,), (1,)))
            s_top = jnp.where(causal, s_top, 0.0).astype(BF16)
            s_diag = jnp.where(causal, s_low[:, mid:], 0.0).astype(BF16)
            s_low = jnp.concatenate([s_low[:, :mid].astype(BF16), s_diag], axis=1)
            top.append(s_top)
            low.append(s_low)
            weights.append(jnp.where(mine, val, zero))
        w_top = jnp.concatenate([w[:mid] for w in weights], axis=0)
        intra_ref[:mid, lanes] = dot(jnp.concatenate(top, axis=1), w_top, ((1,), (0,)))
        w_low = jnp.concatenate(weights, axis=0)
        intra_ref[mid:, lanes] = dot(jnp.concatenate(low, axis=1), w_low, ((1,), (0,)))
    wait_all(loads.values())


def final_kernel(refs, *, slot, places, ext, ready):
    refs = list(refs)
    prior_ref, q_ref, gain_ref = refs[:3]
    refs = refs[3:]
    ext_ref = refs.pop(0) if ext else None
    intra_refs = [refs.pop(0) for _ in range(1 + max(which for which, _ in places))]
    done = [refs.pop(0) for _ in ready]
    out = refs.pop(0)
    part = q_ref.shape[1]
    base = slot_start(slot, part)
    copies = []
    if ready:
        out_hbm, (out, sems) = out, refs
        for n, (other, src) in enumerate(zip(ready, done)):
            there = pl.ds(slot_start(other, part), part)
            copies.append(pltpu.make_async_copy(src, out_hbm.at[:, there], sems.at[1, n]))
            copies[-1].start()
    lane = lax.broadcasted_iota(jnp.int32, (QUAD, QUAD), 1) >> SHIFT
    row = lax.broadcasted_iota(jnp.int32, (QUAD, QUAD), 0) >> SHIFT
    same = lane == row
    ones = jnp.where(same, 1.0 / HEAD_DIM, 0.0).astype(BF16)
    prior = prior_ref[...]
    if ext:
        prior = (prior.astype(F32) + ext_ref[...]).astype(BF16)
    numers = []
    for n, (which, at) in enumerate(places):
        one = prior[n * PAIR : n * PAIR + HEAD_DIM]
        two = prior[n * PAIR + HEAD_DIM : (n + 1) * PAIR]
        block = jnp.concatenate([jnp.concatenate([one, two], axis=1)] * 4, axis=0)
        block = jnp.where(same, block, jnp.zeros_like(block))
        fq = jnp.maximum(q_ref[:, pl.ds(n * QUAD, QUAD)], 0)
        numers.append(dot(fq, block, ((1,), (0,))) + intra_refs[which][:, pl.ds(at, QUAD)])
    for n, numer in enumerate(numers):
        there = pl.ds(pl.multiple_of(base + n * QUAD, QUAD), QUAD)
        lanes = pl.ds(n * QUAD, QUAD)
        mean_sq = dot((numer * numer).astype(BF16), ones, ((1,), (0,)))
        out[:, lanes] = (numer * lax.rsqrt(mean_sq + EPS) * gain_ref[:, there]).astype(BF16)
        if ready:
            copies.append(pltpu.make_async_copy(out.at[:, lanes], out_hbm.at[:, there], sems.at[0, n]))
            copies[-1].start()
    wait_all(copies)


ANY = pl.BlockSpec(memory_space=pl.ANY)
HBM = pl.BlockSpec(memory_space=pltpu.HBM)
VMEM = pl.BlockSpec(memory_space=pltpu.VMEM)
DMA = pltpu.SemaphoreType.DMA


def call(kernel, outs, args, specs=None, out_specs=None, scratch=(), alias=None, cost=(10_000, 10_000)):
    specs = [VMEM] * len(args) if specs is None else specs
    args = [a if s is ANY else pltpu.with_memory_space_constraint(a, s.memory_space) for a, s in zip(args, specs)]
    many = isinstance(outs, (tuple, list))
    return pl.pallas_call(
        kernel,
        out_shape=outs,
        in_specs=specs,
        out_specs=([VMEM] * len(outs) if many else VMEM) if out_specs is None else out_specs,
        scratch_shapes=scratch,
        input_output_aliases=alias or {},
        compiler_params=pltpu.CompilerParams(vmem_limit_bytes=12 * 2**20),
        cost_estimate=pl.CostEstimate(flops=cost[0], transcendentals=0, bytes_accessed=cost[1]),
    )(*args)


def packed(kernel, **static):
    return lambda *refs: kernel(refs, **static)


def on_device(queries, keys, values, gain, *, size):
    count, width = queries.shape
    part = width // 4
    quarter = part // PAIR * HEAD_DIM
    tile = pltpu.VMEM((count, part), BF16)
    k, v, q = [None] * 4, [None] * 4, [None] * 4

    def swap(x, bits):
        return lax.ppermute(x, AXIS, [(i, i ^ bits) for i in range(size)])

    def small(dtype):
        return pltpu.VMEM((quarter, PAIR), dtype)

    send, k[0], v[0], k[2], v[2] = call(
        first_kernel, (small(BF16), *[tile] * 4), (keys, values), specs=[HBM] * 2, scratch=[DMA((4,))]
    )
    got = swap(send, CORE)
    keep, k[1], v[1], k[3], v[3] = call(
        second_kernel,
        (small(F32), *[tile] * 4),
        (keys, values, k[2], v[2]),
        specs=[HBM] * 2 + [VMEM] * 2,
        scratch=[DMA((4,))],
        cost=(80_000_000, 2_000_000),
    )
    send, mine, ext2 = call(after_core, (small(BF16), small(BF16), small(F32)), (keep, got))
    got = swap(send, SIDE)
    send = call(third_kernel, small(BF16), (k[1], v[1]), cost=(80_000_000, 500_000))
    got_core = swap(send, CORE)
    keep, q[2], q[3], gain_vmem = call(
        fourth_kernel,
        (small(F32), tile, tile, pltpu.VMEM((1, width), F32)),
        (k[3], v[3], queries, gain[None, :]),
        specs=[VMEM] * 2 + [HBM] * 2,
        scratch=[DMA((3,))],
        cost=(80_000_000, 1_000_000),
    )
    pairs = width // PAIR
    cuts = (pairs, pairs * 3 // 4, pairs * 3 // 8, 0)
    groups = tuple(zip(cuts[1:], cuts[:-1]))
    parts = []
    for n, (low, high) in enumerate(groups):
        order = tuple(range(high - 1, low - 1, -1))
        slots = tuple(sorted({p * PAIR // part for p in order}))
        fetch = (1, 0) if n == 1 else ()
        args = [queries] if fetch else []
        for slot in slots:
            args += [k[slot], v[slot]]
        args += [q[slot] for slot in slots if slot not in fetch]
        buffer = pltpu.VMEM((count, (high - low) * PAIR), F32)
        outs = call(
            packed(intra_kernel, pairs=order, slots=slots, fetch=fetch),
            (buffer, *[tile] * len(fetch)) if fetch else buffer,
            args,
            specs=[HBM] + [VMEM] * (len(args) - 1) if fetch else None,
            scratch=[DMA((len(fetch),))] if fetch else (),
            cost=(200_000_000, 1_500_000),
        )
        if fetch:
            outs, *found = outs
            for slot, value in zip(fetch, found):
                q[slot] = value
        parts.append(outs)

    send, total, ext_core3, ext_side = call(after_side, (small(BF16), *[small(F32)] * 3), (keep, got_core, got))
    before = []
    level = 2
    while 1 << level < size:
        got = swap(send, 1 << level)
        if 1 << (level + 1) < size:
            more = 1 << (level + 2) < size
            send, *before = call(
                packed(after_outer, level=level, start=not before, more=more),
                (small(BF16), *[small(F32)] * (1 + more)),
                [total, *before, got],
            )
            if more:
                total = before.pop()
        else:
            send, send_core, prior3 = call(
                packed(after_last, level=level, start=not before),
                (small(BF16), small(BF16), small(BF16)),
                [*before, got, ext_side, ext_core3],
            )
        if level == 2:
            ext0 = swap(mine, CORE)
        level += 1
    prior0 = swap(send, CORE | SIDE)
    prior2 = swap(send, SIDE)
    prior1 = swap(send_core, CORE)
    ext0 = call(lambda a, b: b.__setitem__(..., before_core(a)), small(F32), (ext0,))

    ready, done = [], []
    for slot, prior, ext in ((3, prior3, None), (1, prior1, None), (0, prior0, ext0), (2, prior2, ext2)):
        used, places = [], []
        for pair in range(slot * part // PAIR, (slot + 1) * part // PAIR, 2):
            n = next(i for i, (low, high) in enumerate(groups) if low <= pair < high)
            if n not in used:
                used.append(n)
            places.append((used.index(n), (pair - groups[n][0]) * PAIR))
        last = len(ready) == 3
        args = [prior, q[slot], gain_vmem, *([] if ext is None else [ext]), *[parts[n] for n in used]]
        out = call(
            packed(
                final_kernel,
                slot=slot,
                places=tuple(places),
                ext=ext is not None,
                ready=tuple(ready) if last else (),
            ),
            jax.ShapeDtypeStruct((count, width), BF16) if last else tile,
            [*args, *done] if last else args,
            out_specs=ANY if last else None,
            scratch=[tile, DMA((2, 3))] if last else (),
            cost=(50_000_000, 1_000_000),
        )
        ready.append(slot)
        done.append(out)
    return out


def solution(mesh):
    return jax.shard_map(
        functools.partial(on_device, size=mesh.shape[AXIS]),
        mesh=mesh,
        in_specs=(
            P(("groups", "seq"), None),
            P(("groups", "seq"), None),
            P(("groups", "seq"), None),
            P(),
        ),
        out_specs=P(("groups", "seq"), None),
        check_vma=False,
    )
```

```python
import functools

import jax
import jax.numpy as jnp
from jax import lax
from jax.experimental import pallas as pl
from jax.experimental.pallas import tpu as pltpu
from jax.sharding import PartitionSpec as P


HEAD_DIM = 64
PAIR = 2 * HEAD_DIM
QUAD = 4 * HEAD_DIM
SHIFT = 6
CORE, SIDE = 1, 2
EPS = 1e-05
AXIS = "seq"
BF16, F32 = jnp.bfloat16, jnp.float32


def core_bit():
    return lax.axis_index(AXIS) & 1


def side_bit():
    return (lax.axis_index(AXIS) >> 1) & 1


def aligned(index, by):
    return pl.multiple_of(index * by, by)


def first_lanes(shape):
    return lax.broadcasted_iota(jnp.int32, shape, len(shape) - 1) < HEAD_DIM


def dot(a, b, dims):
    return lax.dot_general(a, b, (dims, ((), ())), preferred_element_type=F32)


def slot_start(slot, part):
    core, side = core_bit(), side_bit()
    quarter = 2 * (core if slot >= 2 else 1 - core) + (side if slot % 2 else 1 - side)
    return aligned(quarter, part)


def load_slot(src, dst, slot, sem):
    part = dst.shape[1]
    load = pltpu.make_async_copy(src.at[:, pl.ds(slot_start(slot, part), part)], dst, sem)
    load.start()
    return load


def wait_all(loads):
    for load in loads:
        load.wait()


def states_of(k_ref, v_ref, out_ref):
    first = first_lanes((HEAD_DIM, PAIR))
    for quad in range(k_ref.shape[1] // QUAD):
        lanes = pl.ds(quad * QUAD, QUAD)
        fk = jnp.maximum(k_ref[:, lanes], 0)
        full = dot(fk, v_ref[:, lanes], ((0,), (0,)))
        for p in range(2):
            top = p * PAIR
            rows = full[top : top + PAIR, top : top + PAIR]
            packed = jnp.where(first, rows[:HEAD_DIM], rows[HEAD_DIM:])
            out_ref[pl.ds((quad * 2 + p) * HEAD_DIM, HEAD_DIM), :] = packed.astype(out_ref.dtype)


def first_kernel(k_hbm, v_hbm, send, k0, v0, k2, v2, sems):
    loads = [
        load_slot(src, dst, slot, sems.at[n])
        for n, (src, dst, slot) in enumerate(((k_hbm, k0, 0), (v_hbm, v0, 0), (k_hbm, k2, 2), (v_hbm, v2, 2)))
    ]
    wait_all(loads[:2])
    states_of(k0, v0, send)
    wait_all(loads[2:])


def second_kernel(k_hbm, v_hbm, k2, v2, keep, k1, v1, k3, v3, sems):
    loads = [
        load_slot(src, dst, slot, sems.at[n])
        for n, (src, dst, slot) in enumerate(((k_hbm, k1, 1), (v_hbm, v1, 1), (k_hbm, k3, 3), (v_hbm, v3, 3)))
    ]
    states_of(k2, v2, keep)
    wait_all(loads)


def third_kernel(k1, v1, send):
    states_of(k1, v1, send)


def fourth_kernel(k3, v3, q_hbm, gain_hbm, keep, q2, q3, gain, sems):
    loads = [load_slot(q_hbm, q3, 3, sems.at[0]), load_slot(q_hbm, q2, 2, sems.at[1])]
    loads.append(pltpu.make_async_copy(gain_hbm, gain, sems.at[2]))
    loads[-1].start()
    states_of(k3, v3, keep)
    wait_all(loads)


def before_core(value):
    return jnp.where(core_bit() == 1, value[...].astype(F32), 0.0)


def after_core(keep, got, send, mine, ext):
    send[...] = (keep[...] + got[...].astype(F32)).astype(BF16)
    mine[...] = keep[...].astype(BF16)
    ext[...] = before_core(got)


def after_side(keep, got_core, got, send, total, ext_core, ext_side):
    state, other = keep[...], got_core[...].astype(F32)
    own, from_side = state + other, got[...].astype(F32)
    value = own + from_side
    send[...] = value.astype(BF16)
    total[...] = value
    ext_core[...] = jnp.where(core_bit() == 0, state, other)
    ext_side[...] = jnp.where(side_bit() == 0, own, from_side)


def upper_part(before, got, level):
    upper = (lax.axis_index(AXIS) >> level) & 1
    value = jnp.where(upper == 1, got[...].astype(F32), 0.0)
    return value if before is None else before[...] + value


def after_outer(refs, *, level, start, more):
    refs = list(refs)
    total = refs.pop(0)
    before = None if start else refs.pop(0)
    got, send, before_out, *total_out = refs
    new = total[...] + got[...].astype(F32)
    send[...] = new.astype(BF16)
    before_out[...] = upper_part(before, got, level)
    if more:
        total_out[0][...] = new


def after_last(refs, *, level, start):
    refs = list(refs)
    before = None if start else refs.pop(0)
    got, ext_side, ext_core, send, send_core, prior = refs
    value = upper_part(before, got, level)
    both = value + ext_side[...]
    first = side_bit() == 0
    send[...] = jnp.where(first, both, value).astype(BF16)
    base = jnp.where(first, value, both)
    ahead = base + ext_core[...]
    core = core_bit()
    send_core[...] = jnp.where(core == 0, ahead, base).astype(BF16)
    prior[...] = jnp.where(core == 0, base, ahead).astype(BF16)


def intra_kernel(refs, *, pairs, slots, fetch):
    refs = list(refs)
    q_hbm = refs.pop(0) if fetch else None
    tiles = {slot: [None, refs.pop(0), refs.pop(0)] for slot in slots}
    for slot in slots:
        if slot not in fetch:
            tiles[slot][0] = refs.pop(0)
    intra_ref = refs.pop(0)
    fetched = {slot: refs.pop(0) for slot in fetch}
    loads = {slot: load_slot(q_hbm, ref, slot, refs[-1].at[n]) for n, (slot, ref) in enumerate(fetched.items())}
    for slot in set(fetch) & set(slots):
        tiles[slot][0] = fetched[slot]
    count = intra_ref.shape[0]
    part = tiles[slots[0]][1].shape[1]
    mid = count // 2
    first = first_lanes((count, PAIR))
    rows = lax.broadcasted_iota(jnp.int32, (mid, mid), 0)
    cols = lax.broadcasted_iota(jnp.int32, (mid, mid), 1)
    causal = cols <= rows
    for p in pairs:
        lanes = pl.ds((p - min(pairs)) * PAIR, PAIR)
        slot = p * PAIR // part
        if slot in loads:
            loads.pop(slot).wait()
        q_ref, k_ref, v_ref = tiles[slot]
        there = pl.ds(p * PAIR % part, PAIR)
        fq = jnp.maximum(q_ref[:, there], 0)
        fk = jnp.maximum(k_ref[:, there], 0)
        val = v_ref[:, there]
        zero = jnp.zeros_like(fq)
        top, low, weights = [], [], []
        for h in range(2):
            mine = first if h == 0 else jnp.logical_not(first)
            mine_q = jnp.where(mine, fq, zero)
            s_top = dot(mine_q[:mid], fk[:mid], ((1,), (1,)))
            s_low = dot(mine_q[mid:], fk, ((1,), (1,)))
            s_top = jnp.where(causal, s_top, 0.0).astype(BF16)
            s_diag = jnp.where(causal, s_low[:, mid:], 0.0).astype(BF16)
            s_low = jnp.concatenate([s_low[:, :mid].astype(BF16), s_diag], axis=1)
            top.append(s_top)
            low.append(s_low)
            weights.append(jnp.where(mine, val, zero))
        w_top = jnp.concatenate([w[:mid] for w in weights], axis=0)
        intra_ref[:mid, lanes] = dot(jnp.concatenate(top, axis=1), w_top, ((1,), (0,)))
        w_low = jnp.concatenate(weights, axis=0)
        intra_ref[mid:, lanes] = dot(jnp.concatenate(low, axis=1), w_low, ((1,), (0,)))
    wait_all(loads.values())


def final_kernel(refs, *, slot, places, ext, ready, store, held):
    refs = list(refs)
    prior_ref, q_ref, gain_ref = refs[:3]
    refs = refs[3:]
    ext_ref = refs.pop(0) if ext else None
    intra_refs = [refs.pop(0) for _ in range(1 + max(which for which, _ in places))]
    done = [refs.pop(0) for _ in ready]
    if held:
        refs.pop(0)
    out = refs.pop(0)
    part = q_ref.shape[1]
    base = slot_start(slot, part)
    copies = []
    if store:
        out_hbm, (out, sems) = out, refs
        for n, (other, src) in enumerate(zip(ready, done)):
            there = pl.ds(slot_start(other, part), part)
            copies.append(pltpu.make_async_copy(src, out_hbm.at[:, there], sems.at[1, n]))
            copies[-1].start()
    lane = lax.broadcasted_iota(jnp.int32, (QUAD, QUAD), 1) >> SHIFT
    row = lax.broadcasted_iota(jnp.int32, (QUAD, QUAD), 0) >> SHIFT
    same = lane == row
    ones = jnp.where(same, 1.0 / HEAD_DIM, 0.0).astype(BF16)
    prior = prior_ref[...]
    if ext:
        prior = (prior.astype(F32) + ext_ref[...]).astype(BF16)
    numers = []
    for n, (which, at) in enumerate(places):
        one = prior[n * PAIR : n * PAIR + HEAD_DIM]
        two = prior[n * PAIR + HEAD_DIM : (n + 1) * PAIR]
        block = jnp.concatenate([jnp.concatenate([one, two], axis=1)] * 4, axis=0)
        block = jnp.where(same, block, jnp.zeros_like(block))
        fq = jnp.maximum(q_ref[:, pl.ds(n * QUAD, QUAD)], 0)
        numers.append(dot(fq, block, ((1,), (0,))) + intra_refs[which][:, pl.ds(at, QUAD)])
    for n, numer in enumerate(numers):
        there = pl.ds(pl.multiple_of(base + n * QUAD, QUAD), QUAD)
        lanes = pl.ds(n * QUAD, QUAD)
        mean_sq = dot((numer * numer).astype(BF16), ones, ((1,), (0,)))
        out[:, lanes] = (numer * lax.rsqrt(mean_sq + EPS) * gain_ref[:, there]).astype(BF16)
        if store:
            copies.append(pltpu.make_async_copy(out.at[:, lanes], out_hbm.at[:, there], sems.at[0, n]))
            copies[-1].start()
    wait_all(copies)


ANY = pl.BlockSpec(memory_space=pl.ANY)
HBM = pl.BlockSpec(memory_space=pltpu.HBM)
VMEM = pl.BlockSpec(memory_space=pltpu.VMEM)
DMA = pltpu.SemaphoreType.DMA


def call(kernel, outs, args, specs=None, out_specs=None, scratch=(), alias=None, cost=(10_000, 10_000)):
    specs = [VMEM] * len(args) if specs is None else specs
    args = [a if s is ANY else pltpu.with_memory_space_constraint(a, s.memory_space) for a, s in zip(args, specs)]
    many = isinstance(outs, (tuple, list))
    return pl.pallas_call(
        kernel,
        out_shape=outs,
        in_specs=specs,
        out_specs=([VMEM] * len(outs) if many else VMEM) if out_specs is None else out_specs,
        scratch_shapes=scratch,
        input_output_aliases=alias or {},
        compiler_params=pltpu.CompilerParams(vmem_limit_bytes=12 * 2**20),
        cost_estimate=pl.CostEstimate(flops=cost[0], transcendentals=0, bytes_accessed=cost[1]),
    )(*args)


def packed(kernel, **static):
    return lambda *refs: kernel(refs, **static)


def on_device(queries, keys, values, gain, *, size):
    count, width = queries.shape
    part = width // 4
    quarter = part // PAIR * HEAD_DIM
    tile = pltpu.VMEM((count, part), BF16)
    k, v, q = [None] * 4, [None] * 4, [None] * 4

    def swap(x, bits):
        return lax.ppermute(x, AXIS, [(i, i ^ bits) for i in range(size)])

    def small(dtype):
        return pltpu.VMEM((quarter, PAIR), dtype)

    send, k[0], v[0], k[2], v[2] = call(
        first_kernel, (small(BF16), *[tile] * 4), (keys, values), specs=[HBM] * 2, scratch=[DMA((4,))]
    )
    got = swap(send, CORE)
    keep, k[1], v[1], k[3], v[3] = call(
        second_kernel,
        (small(F32), *[tile] * 4),
        (keys, values, k[2], v[2]),
        specs=[HBM] * 2 + [VMEM] * 2,
        scratch=[DMA((4,))],
        cost=(80_000_000, 2_000_000),
    )
    send, mine, ext2 = call(after_core, (small(BF16), small(BF16), small(F32)), (keep, got))
    got = swap(send, SIDE)
    send = call(third_kernel, small(BF16), (k[1], v[1]), cost=(80_000_000, 500_000))
    got_core = swap(send, CORE)
    keep, q[2], q[3], gain_vmem = call(
        fourth_kernel,
        (small(F32), tile, tile, pltpu.VMEM((1, width), F32)),
        (k[3], v[3], queries, gain[None, :]),
        specs=[VMEM] * 2 + [HBM] * 2,
        scratch=[DMA((3,))],
        cost=(80_000_000, 1_000_000),
    )
    pairs = width // PAIR
    cuts = (pairs, pairs * 3 // 4, pairs * 3 // 8, 0)
    groups = tuple(zip(cuts[1:], cuts[:-1]))
    parts = []
    for n, (low, high) in enumerate(groups):
        order = tuple(range(high - 1, low - 1, -1))
        slots = tuple(sorted({p * PAIR // part for p in order}))
        fetch = (1, 0) if n == 1 else ()
        args = [queries] if fetch else []
        for slot in slots:
            args += [k[slot], v[slot]]
        args += [q[slot] for slot in slots if slot not in fetch]
        buffer = pltpu.VMEM((count, (high - low) * PAIR), F32)
        outs = call(
            packed(intra_kernel, pairs=order, slots=slots, fetch=fetch),
            (buffer, *[tile] * len(fetch)) if fetch else buffer,
            args,
            specs=[HBM] + [VMEM] * (len(args) - 1) if fetch else None,
            scratch=[DMA((len(fetch),))] if fetch else (),
            cost=(200_000_000, 1_500_000),
        )
        if fetch:
            outs, *found = outs
            for slot, value in zip(fetch, found):
                q[slot] = value
        parts.append(outs)

    send, total, ext_core3, ext_side = call(after_side, (small(BF16), *[small(F32)] * 3), (keep, got_core, got))
    before = []
    level = 2
    while 1 << level < size:
        got = swap(send, 1 << level)
        if 1 << (level + 1) < size:
            more = 1 << (level + 2) < size
            send, *before = call(
                packed(after_outer, level=level, start=not before, more=more),
                (small(BF16), *[small(F32)] * (1 + more)),
                [total, *before, got],
            )
            if more:
                total = before.pop()
        else:
            send, send_core, prior3 = call(
                packed(after_last, level=level, start=not before),
                (small(BF16), small(BF16), small(BF16)),
                [*before, got, ext_side, ext_core3],
            )
        if level == 2:
            ext0 = swap(mine, CORE)
        level += 1
    prior2 = swap(send, SIDE)
    prior0 = swap(send, CORE | SIDE)
    prior1 = swap(send_core, CORE)
    ext0 = call(lambda a, b: b.__setitem__(..., before_core(a)), small(F32), (ext0,))

    out, ready, done, waiting = None, [], [], []
    for slot, prior, ext in ((3, prior3, None), (1, prior1, None), (2, prior2, ext2), (0, prior0, ext0)):
        used, places = [], []
        for pair in range(slot * part // PAIR, (slot + 1) * part // PAIR, 2):
            n = next(i for i, (low, high) in enumerate(groups) if low <= pair < high)
            if n not in used:
                used.append(n)
            places.append((used.index(n), (pair - groups[n][0]) * PAIR))
        store = slot % 2 == 0
        args = [prior, q[slot], gain_vmem, *([] if ext is None else [ext]), *[parts[n] for n in used], *done]
        specs = [VMEM] * len(args)
        alias = {}
        if out is not None:
            alias = {len(args): 0}
            args, specs = [*args, out], [*specs, ANY]
        result = call(
            packed(
                final_kernel,
                slot=slot,
                places=tuple(places),
                ext=ext is not None,
                ready=tuple(ready),
                store=store,
                held=out is not None,
            ),
            jax.ShapeDtypeStruct((count, width), BF16) if store else tile,
            args,
            specs=specs,
            out_specs=ANY if store else None,
            scratch=[tile, DMA((2, 3))] if store else (),
            alias=alias,
            cost=(50_000_000, 1_000_000),
        )
        if store:
            out, ready, done = result, [], []
        else:
            waiting.append((slot, result))
            if len(waiting) == 2:
                ready, done = [list(x) for x in zip(*waiting)]
    return out


def solution(mesh):
    return jax.shard_map(
        functools.partial(on_device, size=mesh.shape[AXIS]),
        mesh=mesh,
        in_specs=(
            P(("groups", "seq"), None),
            P(("groups", "seq"), None),
            P(("groups", "seq"), None),
            P(),
        ),
        out_specs=P(("groups", "seq"), None),
        check_vma=False,
    )
```

```python
import functools

import jax
import jax.numpy as jnp
from jax import lax
from jax.experimental import pallas as pl
from jax.experimental.pallas import tpu as pltpu
from jax.sharding import PartitionSpec as P


HEAD_DIM = 64
PAIR = 2 * HEAD_DIM
QUAD = 4 * HEAD_DIM
SHIFT = 6
CORE, SIDE = 1, 2
EPS = 1e-05
AXIS = "seq"
BF16, F32 = jnp.bfloat16, jnp.float32


def bit_of(level):
    return (lax.axis_index(AXIS) >> level) & 1


def first_lanes(shape):
    return lax.broadcasted_iota(jnp.int32, shape, len(shape) - 1) < HEAD_DIM


def dot(a, b, dims):
    return lax.dot_general(a, b, (dims, ((), ())), preferred_element_type=F32)


def half_start(own, half):
    core = bit_of(0)
    return pl.multiple_of((core if own else 1 - core) * half, half)


def load_half(src, dst, own, sem, start=0, width=None):
    half = dst.shape[1]
    width = half if width is None else width
    there = pl.ds(pl.multiple_of(half_start(own, half) + start, width), width)
    load = pltpu.make_async_copy(src.at[:, there], dst.at[:, pl.ds(start, width)], sem)
    load.start()
    return load


def wait_all(loads):
    for load in loads:
        load.wait()


def states_of(k_ref, v_ref, out_ref, quads):
    first = first_lanes((HEAD_DIM, PAIR))
    for quad in quads:
        lanes = pl.ds(quad * QUAD, QUAD)
        fk = jnp.maximum(k_ref[:, lanes], 0)
        full = dot(fk, v_ref[:, lanes], ((0,), (0,)))
        for p in range(2):
            top = p * PAIR
            rows = full[top : top + PAIR, top : top + PAIR]
            packed = jnp.where(first, rows[:HEAD_DIM], rows[HEAD_DIM:])
            out_ref[pl.ds((quad * 2 + p) * HEAD_DIM, HEAD_DIM), :] = packed.astype(out_ref.dtype)


def first_kernel(k_hbm, v_hbm, send, k_other, v_other, k_own, v_own, sems):
    half = k_other.shape[1]
    part = half // 2
    loads = []
    for n in range(2):
        for m, (src, dst) in enumerate(((k_hbm, k_other), (v_hbm, v_other))):
            loads.append(load_half(src, dst, False, sems.at[n, m], n * part, part))
    late = [load_half(src, dst, True, sems.at[2, m]) for m, (src, dst) in enumerate(((k_hbm, k_own), (v_hbm, v_own)))]
    quads = part // QUAD
    for n in range(2):
        wait_all(loads[2 * n : 2 * n + 2])
        states_of(k_other, v_other, send, range(n * quads, (n + 1) * quads))
    wait_all(late)


def second_kernel(k_own, v_own, q_hbm, gain_hbm, keep, q_own, gain, sems):
    loads = [load_half(q_hbm, q_own, True, sems.at[0]), pltpu.make_async_copy(gain_hbm, gain, sems.at[1])]
    loads[1].start()
    states_of(k_own, v_own, keep, range(k_own.shape[1] // QUAD))
    wait_all(loads)


def after_core(keep, got, send, total, ext):
    state, other = keep[...], got[...].astype(F32)
    value = state + other
    send[...] = value.astype(BF16)
    total[...] = value
    ext[...] = jnp.where(bit_of(0) == 0, state, other)


def later_of(n, rounds):
    low = bit_of(1 + n)
    return jnp.where(bit_of(0) == 0, low, bit_of(2 + n)) if n + 1 < rounds else low


def with_got(before, got, n, rounds):
    value = got[...].astype(F32)
    taken = later_of(n, rounds) == 1
    if n + 1 == rounds:
        taken = jnp.logical_or(taken, bit_of(0) == 1)
    value = jnp.where(taken, value, 0.0)
    return value if before is None else before[...] + value


def after_round(refs, *, n, rounds):
    refs = list(refs)
    before = refs.pop(0) if n else None
    total, got, *refs = refs
    sent = total[...] + got[...].astype(F32)
    value = with_got(before, got, n, rounds)
    if n + 2 == rounds:
        chip, send, before_out = refs
        share = value + jnp.where(bit_of(1) == 0, chip[...], 0.0)
        send[...] = jnp.where(bit_of(0) == 0, sent, share).astype(BF16)
    else:
        send, before_out, total_out = refs
        send[...] = sent.astype(BF16)
        total_out[...] = sent
    before_out[...] = value


def after_last(before, got, ext, send, prior, *, n, rounds):
    base = with_got(before, got, n, rounds)
    ahead = base + ext[...]
    first = bit_of(0) == 0
    send[...] = jnp.where(first, ahead, base).astype(BF16)
    prior[...] = jnp.where(first, base, ahead).astype(BF16)


def intra_kernel(refs, *, fetch):
    q_hbm = refs[0] if fetch else None
    q_ref, k_ref, v_ref, intra_ref, *refs = refs[1:] if fetch else refs
    loads = [load_half(q_hbm, refs[0], False, refs[1].at[0])] if fetch else []
    count, half = intra_ref.shape
    mid = count // 2
    first = first_lanes((count, PAIR))
    rows = lax.broadcasted_iota(jnp.int32, (mid, mid), 0)
    cols = lax.broadcasted_iota(jnp.int32, (mid, mid), 1)
    causal = cols <= rows
    for p in range(half // PAIR):
        lanes = pl.ds(p * PAIR, PAIR)
        fq = jnp.maximum(q_ref[:, lanes], 0)
        fk = jnp.maximum(k_ref[:, lanes], 0)
        val = v_ref[:, lanes]
        zero = jnp.zeros_like(fq)
        top, low, weights = [], [], []
        for h in range(2):
            mine = first if h == 0 else jnp.logical_not(first)
            mine_q = jnp.where(mine, fq, zero)
            s_top = dot(mine_q[:mid], fk[:mid], ((1,), (1,)))
            s_low = dot(mine_q[mid:], fk, ((1,), (1,)))
            s_top = jnp.where(causal, s_top, 0.0).astype(BF16)
            s_diag = jnp.where(causal, s_low[:, mid:], 0.0).astype(BF16)
            s_low = jnp.concatenate([s_low[:, :mid].astype(BF16), s_diag], axis=1)
            top.append(s_top)
            low.append(s_low)
            weights.append(jnp.where(mine, val, zero))
        w_top = jnp.concatenate([w[:mid] for w in weights], axis=0)
        intra_ref[:mid, lanes] = dot(jnp.concatenate(top, axis=1), w_top, ((1,), (0,)))
        w_low = jnp.concatenate(weights, axis=0)
        intra_ref[mid:, lanes] = dot(jnp.concatenate(low, axis=1), w_low, ((1,), (0,)))
    wait_all(loads)


def final_kernel(refs, *, own):
    prior_ref, q_ref, gain_ref, intra_ref = refs[:4]
    out_hbm, out_buf, sems = refs[-3:]
    half = out_buf.shape[1]
    base = half_start(own, half)
    lane = lax.broadcasted_iota(jnp.int32, (QUAD, QUAD), 1) >> SHIFT
    row = lax.broadcasted_iota(jnp.int32, (QUAD, QUAD), 0) >> SHIFT
    same = lane == row
    ones = jnp.where(same, 1.0 / HEAD_DIM, 0.0).astype(BF16)
    copies = []
    GROUP = 2
    for start in range(0, half // QUAD, GROUP):
        numers = []
        for n in range(start, start + GROUP):
            one = prior_ref[pl.ds(n * PAIR, HEAD_DIM), :]
            two = prior_ref[pl.ds(n * PAIR + HEAD_DIM, HEAD_DIM), :]
            block = jnp.concatenate([jnp.concatenate([one, two], axis=1)] * 4, axis=0)
            block = jnp.where(same, block, jnp.zeros_like(block))
            lanes = pl.ds(n * QUAD, QUAD)
            fq = jnp.maximum(q_ref[:, lanes], 0)
            numers.append(dot(fq, block, ((1,), (0,))) + intra_ref[:, lanes])
        for n, numer in enumerate(numers, start):
            lanes = pl.ds(n * QUAD, QUAD)
            there = pl.ds(pl.multiple_of(base + n * QUAD, QUAD), QUAD)
            mean_sq = dot((numer * numer).astype(BF16), ones, ((1,), (0,)))
            out_buf[:, lanes] = (numer * lax.rsqrt(mean_sq + EPS) * gain_ref[:, there]).astype(BF16)
            copies.append(pltpu.make_async_copy(out_buf.at[:, lanes], out_hbm.at[:, there], sems.at[n]))
            copies[-1].start()
    wait_all(copies)


ANY = pl.BlockSpec(memory_space=pl.ANY)
HBM = pl.BlockSpec(memory_space=pltpu.HBM)
VMEM = pl.BlockSpec(memory_space=pltpu.VMEM)
DMA = pltpu.SemaphoreType.DMA


def call(kernel, outs, args, specs=None, out_specs=None, scratch=(), alias=None, cost=(10_000, 10_000)):
    specs = [VMEM] * len(args) if specs is None else specs
    args = [a if s is ANY else pltpu.with_memory_space_constraint(a, s.memory_space) for a, s in zip(args, specs)]
    many = isinstance(outs, (tuple, list))
    return pl.pallas_call(
        kernel,
        out_shape=outs,
        in_specs=specs,
        out_specs=([VMEM] * len(outs) if many else VMEM) if out_specs is None else out_specs,
        scratch_shapes=scratch,
        input_output_aliases=alias or {},
        compiler_params=pltpu.CompilerParams(vmem_limit_bytes=12 * 2**20),
        cost_estimate=pl.CostEstimate(flops=cost[0], transcendentals=0, bytes_accessed=cost[1]),
    )(*args)


def packed(kernel, **static):
    return lambda *refs: kernel(refs, **static)


def on_device(queries, keys, values, gain, *, size):
    count, width = queries.shape
    half = width // 2
    rows = half // PAIR * HEAD_DIM
    rounds = size.bit_length() - 2
    tile = pltpu.VMEM((count, half), BF16)
    small16, small32 = pltpu.VMEM((rows, PAIR), BF16), pltpu.VMEM((rows, PAIR), F32)

    def swap(x, even, odd):
        return lax.ppermute(x, AXIS, [(i, i ^ (odd if i & CORE else even)) for i in range(size)])

    send, k_other, v_other, k_own, v_own = call(
        first_kernel, (small16, *[tile] * 4), (keys, values), specs=[HBM] * 2, scratch=[DMA((3, 2))]
    )
    got = swap(send, CORE, CORE)
    keep, q_own, gain_vmem = call(
        second_kernel,
        (small32, tile, pltpu.VMEM((1, width), F32)),
        (k_own, v_own, queries, gain[None, :]),
        specs=[VMEM] * 2 + [HBM] * 2,
        scratch=[DMA((2,))],
        cost=(150_000_000, 2_000_000),
    )
    scores = pltpu.VMEM((count, half), F32)
    intra_own, q_other = call(
        packed(intra_kernel, fetch=True),
        (scores, tile),
        (queries, q_own, k_own, v_own),
        specs=[HBM] + [VMEM] * 3,
        scratch=[DMA((1,))],
        cost=(300_000_000, 2_000_000),
    )
    intra_other = call(
        packed(intra_kernel, fetch=False), scores, (q_other, k_other, v_other), cost=(300_000_000, 2_000_000)
    )

    send, chip, ext = call(after_core, (small16, small32, small32), (keep, got))
    total, before = chip, []
    for n in range(rounds):
        odd = 2 << (n + 1) if n + 1 < rounds else SIDE
        got = swap(send, SIDE << n, odd)
        if n + 1 == rounds:
            break
        last = n + 2 == rounds
        send, *before = call(
            packed(after_round, n=n, rounds=rounds),
            (small16, *[small32] * (1 if last else 2)),
            [*before[:1], total, got, *([chip] if last else [])],
        )
        if not last:
            total = before.pop()
    send, prior = call(
        functools.partial(after_last, n=rounds - 1, rounds=rounds), (small16, small16), [*before, got, ext]
    )
    got = swap(send, CORE, CORE)

    out = None
    for own, prior, q, intra in ((True, prior, q_own, intra_own), (False, got, q_other, intra_other)):
        args = [prior, q, gain_vmem, intra]
        specs = [VMEM] * 4
        alias = {}
        if out is not None:
            args, specs, alias = [*args, out], [*specs, ANY], {4: 0}
        out = call(
            packed(final_kernel, own=own),
            jax.ShapeDtypeStruct((count, width), BF16),
            args,
            specs=specs,
            out_specs=ANY,
            scratch=[tile, DMA((half // QUAD,))],
            alias=alias,
            cost=(100_000_000, 2_000_000),
        )
    return out


def solution(mesh):
    return jax.shard_map(
        functools.partial(on_device, size=mesh.shape[AXIS]),
        mesh=mesh,
        in_specs=(
            P(("groups", "seq"), None),
            P(("groups", "seq"), None),
            P(("groups", "seq"), None),
            P(),
        ),
        out_specs=P(("groups", "seq"), None),
        check_vma=False,
    )
```

```python
import functools

import jax
import jax.numpy as jnp
from jax import lax
from jax.experimental import pallas as pl
from jax.experimental.pallas import tpu as pltpu
from jax.sharding import PartitionSpec as P


HEAD_DIM = 64
PAIR = 2 * HEAD_DIM
QUAD = 4 * HEAD_DIM
SHIFT = 6
CORE, SIDE = 1, 2
EPS = 1e-05
AXIS = "seq"
BF16, F32 = jnp.bfloat16, jnp.float32


def bit_of(level):
    return (lax.axis_index(AXIS) >> level) & 1


def first_lanes(shape):
    return lax.broadcasted_iota(jnp.int32, shape, len(shape) - 1) < HEAD_DIM


def dot(a, b, dims):
    return lax.dot_general(a, b, (dims, ((), ())), preferred_element_type=F32)


def half_start(own, half):
    core = bit_of(0)
    return pl.multiple_of((core if own else 1 - core) * half, half)


def load_half(src, dst, own, sem, start=0, width=None):
    half = dst.shape[1]
    width = half if width is None else width
    there = pl.ds(pl.multiple_of(half_start(own, half) + start, width), width)
    load = pltpu.make_async_copy(src.at[:, there], dst.at[:, pl.ds(start, width)], sem)
    load.start()
    return load


def wait_all(loads):
    for load in loads:
        load.wait()


def states_of(k_ref, v_ref, out_ref, quads):
    first = first_lanes((HEAD_DIM, PAIR))
    for quad in quads:
        lanes = pl.ds(quad * QUAD, QUAD)
        fk = jnp.maximum(k_ref[:, lanes], 0)
        full = dot(fk, v_ref[:, lanes], ((0,), (0,)))
        for p in range(2):
            top = p * PAIR
            rows = full[top : top + PAIR, top : top + PAIR]
            packed = jnp.where(first, rows[:HEAD_DIM], rows[HEAD_DIM:])
            out_ref[pl.ds((quad * 2 + p) * HEAD_DIM, HEAD_DIM), :] = packed.astype(out_ref.dtype)


def first_kernel(k_hbm, v_hbm, send, k_other, v_other, k_own, v_own, sems):
    half = k_other.shape[1]
    part = half // 2
    loads = []
    for n in range(2):
        for m, (src, dst) in enumerate(((k_hbm, k_other), (v_hbm, v_other))):
            loads.append(load_half(src, dst, False, sems.at[n, m], n * part, part))
    late = [load_half(src, dst, True, sems.at[2, m]) for m, (src, dst) in enumerate(((k_hbm, k_own), (v_hbm, v_own)))]
    quads = part // QUAD
    for n in range(2):
        wait_all(loads[2 * n : 2 * n + 2])
        states_of(k_other, v_other, send, range(n * quads, (n + 1) * quads))
    wait_all(late)


def second_kernel(k_own, v_own, q_hbm, gain_hbm, keep, q_own, gain, sems):
    loads = [load_half(q_hbm, q_own, True, sems.at[0]), pltpu.make_async_copy(gain_hbm, gain, sems.at[1])]
    loads[1].start()
    states_of(k_own, v_own, keep, range(k_own.shape[1] // QUAD))
    wait_all(loads)


def after_core(keep, got, send, total, ext):
    state, other = keep[...], got[...].astype(F32)
    value = state + other
    send[...] = value.astype(BF16)
    total[...] = value
    ext[...] = jnp.where(bit_of(0) == 0, state, other)


def later_of(n, rounds):
    low = bit_of(1 + n)
    return jnp.where(bit_of(0) == 0, low, bit_of(2 + n)) if n + 1 < rounds else low


def with_got(before, got, n, rounds):
    value = got[...].astype(F32)
    taken = later_of(n, rounds) == 1
    if n + 1 == rounds:
        taken = jnp.logical_or(taken, bit_of(0) == 1)
    value = jnp.where(taken, value, 0.0)
    return value if before is None else before[...] + value


def after_round(refs, *, n, rounds):
    refs = list(refs)
    before = refs.pop(0) if n else None
    total, got, *refs = refs
    sent = total[...] + got[...].astype(F32)
    value = with_got(before, got, n, rounds)
    if n + 2 == rounds:
        chip, send, before_out = refs
        share = value + jnp.where(bit_of(1) == 0, chip[...], 0.0)
        send[...] = jnp.where(bit_of(0) == 0, sent, share).astype(BF16)
    else:
        send, before_out, total_out = refs
        send[...] = sent.astype(BF16)
        total_out[...] = sent
    before_out[...] = value


def after_last(before, got, ext, send0, send1, prior, *, n, rounds):
    base = with_got(before, got, n, rounds)
    ahead = base + ext[...]
    first = bit_of(0) == 0
    send = jnp.where(first, ahead, base).astype(BF16)
    send0[...] = send[: send0.shape[0]]
    send1[...] = send[send0.shape[0] :]
    prior[...] = jnp.where(first, base, ahead).astype(BF16)


def intra_kernel(refs, *, fetch):
    q_hbm = refs[0] if fetch else None
    q_ref, k_ref, v_ref, intra_ref, *refs = refs[1:] if fetch else refs
    loads = [load_half(q_hbm, refs[0], False, refs[1].at[0])] if fetch else []
    count, half = intra_ref.shape
    mid = count // 2
    first = first_lanes((count, PAIR))
    rows = lax.broadcasted_iota(jnp.int32, (mid, mid), 0)
    cols = lax.broadcasted_iota(jnp.int32, (mid, mid), 1)
    causal = cols <= rows
    for p in range(half // PAIR):
        lanes = pl.ds(p * PAIR, PAIR)
        fq = jnp.maximum(q_ref[:, lanes], 0)
        fk = jnp.maximum(k_ref[:, lanes], 0)
        val = v_ref[:, lanes]
        zero = jnp.zeros_like(fq)
        top, low, weights = [], [], []
        for h in range(2):
            mine = first if h == 0 else jnp.logical_not(first)
            mine_q = jnp.where(mine, fq, zero)
            s_top = dot(mine_q[:mid], fk[:mid], ((1,), (1,)))
            s_low = dot(mine_q[mid:], fk, ((1,), (1,)))
            s_top = jnp.where(causal, s_top, 0.0).astype(BF16)
            s_diag = jnp.where(causal, s_low[:, mid:], 0.0).astype(BF16)
            s_low = jnp.concatenate([s_low[:, :mid].astype(BF16), s_diag], axis=1)
            top.append(s_top)
            low.append(s_low)
            weights.append(jnp.where(mine, val, zero))
        w_top = jnp.concatenate([w[:mid] for w in weights], axis=0)
        intra_ref[:mid, lanes] = dot(jnp.concatenate(top, axis=1), w_top, ((1,), (0,)))
        w_low = jnp.concatenate(weights, axis=0)
        intra_ref[mid:, lanes] = dot(jnp.concatenate(low, axis=1), w_low, ((1,), (0,)))
    wait_all(loads)


def final_kernel(refs, *, own, at, last):
    refs = list(refs)
    prior_ref, q_ref, gain_ref, intra_ref = refs[:4]
    half = q_ref.shape[1]
    base = half_start(own, half) + at
    copies = []
    if last:
        own_ref, part_ref, out_hbm, out, sems = refs[4:]
        own_lanes = pl.ds(half_start(True, half), half)
        copies.append(pltpu.make_async_copy(own_ref, out_hbm.at[:, own_lanes], sems.at[0]))
        part_lanes = pl.ds(half_start(False, half), part_ref.shape[1])
        copies.append(pltpu.make_async_copy(part_ref, out_hbm.at[:, part_lanes], sems.at[1]))
        for copy in copies:
            copy.start()
    else:
        out = refs[4]
    width = out.shape[1]
    lane = lax.broadcasted_iota(jnp.int32, (QUAD, QUAD), 1) >> SHIFT
    row = lax.broadcasted_iota(jnp.int32, (QUAD, QUAD), 0) >> SHIFT
    same = lane == row
    ones = jnp.where(same, 1.0 / HEAD_DIM, 0.0).astype(BF16)
    for start in range(0, width // QUAD, 2):
        numers = []
        for n in range(start, start + 2):
            one = prior_ref[pl.ds(n * PAIR, HEAD_DIM), :]
            two = prior_ref[pl.ds(n * PAIR + HEAD_DIM, HEAD_DIM), :]
            block = jnp.concatenate([jnp.concatenate([one, two], axis=1)] * 4, axis=0)
            block = jnp.where(same, block, jnp.zeros_like(block))
            lanes = pl.ds(at + n * QUAD, QUAD)
            fq = jnp.maximum(q_ref[:, lanes], 0)
            numers.append(dot(fq, block, ((1,), (0,))) + intra_ref[:, lanes])
        for n, numer in enumerate(numers, start):
            lanes = pl.ds(n * QUAD, QUAD)
            there = pl.ds(pl.multiple_of(base + n * QUAD, QUAD), QUAD)
            mean_sq = dot((numer * numer).astype(BF16), ones, ((1,), (0,)))
            out[:, lanes] = (numer * lax.rsqrt(mean_sq + EPS) * gain_ref[:, there]).astype(BF16)
            if last:
                copies.append(pltpu.make_async_copy(out.at[:, lanes], out_hbm.at[:, there], sems.at[2 + n]))
                copies[-1].start()
    wait_all(copies)


ANY = pl.BlockSpec(memory_space=pl.ANY)
HBM = pl.BlockSpec(memory_space=pltpu.HBM)
VMEM = pl.BlockSpec(memory_space=pltpu.VMEM)
DMA = pltpu.SemaphoreType.DMA


def call(kernel, outs, args, specs=None, out_specs=None, scratch=(), alias=None, cost=(10_000, 10_000)):
    specs = [VMEM] * len(args) if specs is None else specs
    args = [a if s is ANY else pltpu.with_memory_space_constraint(a, s.memory_space) for a, s in zip(args, specs)]
    many = isinstance(outs, (tuple, list))
    return pl.pallas_call(
        kernel,
        out_shape=outs,
        in_specs=specs,
        out_specs=([VMEM] * len(outs) if many else VMEM) if out_specs is None else out_specs,
        scratch_shapes=scratch,
        input_output_aliases=alias or {},
        compiler_params=pltpu.CompilerParams(vmem_limit_bytes=12 * 2**20),
        cost_estimate=pl.CostEstimate(flops=cost[0], transcendentals=0, bytes_accessed=cost[1]),
    )(*args)


def packed(kernel, **static):
    return lambda *refs: kernel(refs, **static)


def on_device(queries, keys, values, gain, *, size):
    count, width = queries.shape
    half = width // 2
    rows = half // PAIR * HEAD_DIM
    rounds = size.bit_length() - 2
    tile = pltpu.VMEM((count, half), BF16)
    small16, small32 = pltpu.VMEM((rows, PAIR), BF16), pltpu.VMEM((rows, PAIR), F32)

    def swap(x, even, odd):
        return lax.ppermute(x, AXIS, [(i, i ^ (odd if i & CORE else even)) for i in range(size)])

    send, k_other, v_other, k_own, v_own = call(
        first_kernel, (small16, *[tile] * 4), (keys, values), specs=[HBM] * 2, scratch=[DMA((3, 2))]
    )
    got = swap(send, CORE, CORE)
    keep, q_own, gain_vmem = call(
        second_kernel,
        (small32, tile, pltpu.VMEM((1, width), F32)),
        (k_own, v_own, queries, gain[None, :]),
        specs=[VMEM] * 2 + [HBM] * 2,
        scratch=[DMA((2,))],
        cost=(150_000_000, 2_000_000),
    )
    scores = pltpu.VMEM((count, half), F32)
    intra_own, q_other = call(
        packed(intra_kernel, fetch=True),
        (scores, tile),
        (queries, q_own, k_own, v_own),
        specs=[HBM] + [VMEM] * 3,
        scratch=[DMA((1,))],
        cost=(300_000_000, 2_000_000),
    )
    intra_other = call(
        packed(intra_kernel, fetch=False), scores, (q_other, k_other, v_other), cost=(300_000_000, 2_000_000)
    )

    send, chip, ext = call(after_core, (small16, small32, small32), (keep, got))
    total, before = chip, []
    for n in range(rounds):
        odd = 2 << (n + 1) if n + 1 < rounds else SIDE
        got = swap(send, SIDE << n, odd)
        if n + 1 == rounds:
            break
        last = n + 2 == rounds
        send, *before = call(
            packed(after_round, n=n, rounds=rounds),
            (small16, *[small32] * (1 if last else 2)),
            [*before[:1], total, got, *([chip] if last else [])],
        )
        if not last:
            total = before.pop()
    quarter = pltpu.VMEM((rows // 2, PAIR), BF16)
    send0, send1, prior = call(
        functools.partial(after_last, n=rounds - 1, rounds=rounds), (quarter, quarter, small16), [*before, got, ext]
    )
    got0 = swap(send0, CORE, CORE)
    got1 = swap(send1, CORE, CORE)

    part = half // 2
    left = pltpu.VMEM((count, part), BF16)
    cost = (100_000_000, 2_000_000)
    done_own = call(
        packed(final_kernel, own=True, at=0, last=False), tile, (prior, q_own, gain_vmem, intra_own), cost=cost
    )
    done_part = call(
        packed(final_kernel, own=False, at=0, last=False), left, (got0, q_other, gain_vmem, intra_other), cost=cost
    )
    return call(
        packed(final_kernel, own=False, at=part, last=True),
        jax.ShapeDtypeStruct((count, width), BF16),
        (got1, q_other, gain_vmem, intra_other, done_own, done_part),
        out_specs=ANY,
        scratch=[left, DMA((2 + part // QUAD,))],
        cost=cost,
    )


def solution(mesh):
    return jax.shard_map(
        functools.partial(on_device, size=mesh.shape[AXIS]),
        mesh=mesh,
        in_specs=(
            P(("groups", "seq"), None),
            P(("groups", "seq"), None),
            P(("groups", "seq"), None),
            P(),
        ),
        out_specs=P(("groups", "seq"), None),
        check_vma=False,
    )
```

```python
import functools

import jax
import jax.numpy as jnp
from jax import lax
from jax.experimental import pallas as pl
from jax.experimental.pallas import tpu as pltpu
from jax.sharding import PartitionSpec as P


HEAD_DIM = 64
PAIR = 2 * HEAD_DIM
QUAD = 4 * HEAD_DIM
SHIFT = 6
CORE, SIDE = 1, 2
EPS = 1e-05
AXIS = "seq"
BF16, F32 = jnp.bfloat16, jnp.float32


def bit_of(level):
    return (lax.axis_index(AXIS) >> level) & 1


def first_lanes(shape):
    return lax.broadcasted_iota(jnp.int32, shape, len(shape) - 1) < HEAD_DIM


def dot(a, b, dims):
    return lax.dot_general(a, b, (dims, ((), ())), preferred_element_type=F32)


def half_start(own, half):
    core = bit_of(0)
    return pl.multiple_of((core if own else 1 - core) * half, half)


def load_half(src, dst, own, sem, start=0, width=None):
    half = dst.shape[1]
    width = half if width is None else width
    there = pl.ds(pl.multiple_of(half_start(own, half) + start, width), width)
    load = pltpu.make_async_copy(src.at[:, there], dst.at[:, pl.ds(start, width)], sem)
    load.start()
    return load


def wait_all(loads):
    for load in loads:
        load.wait()


def states_of(k_ref, v_ref, out_ref, quads):
    first = first_lanes((HEAD_DIM, PAIR))
    for quad in quads:
        lanes = pl.ds(quad * QUAD, QUAD)
        fk = jnp.maximum(k_ref[:, lanes], 0)
        full = dot(fk, v_ref[:, lanes], ((0,), (0,)))
        for p in range(2):
            top = p * PAIR
            rows = full[top : top + PAIR, top : top + PAIR]
            packed = jnp.where(first, rows[:HEAD_DIM], rows[HEAD_DIM:])
            out_ref[pl.ds((quad * 2 + p) * HEAD_DIM, HEAD_DIM), :] = packed.astype(out_ref.dtype)


def first_kernel(k_hbm, v_hbm, send, k_other, v_other, k_own, v_own, sems):
    half = k_other.shape[1]
    part = half // 2
    loads = []
    for n in range(2):
        for m, (src, dst) in enumerate(((k_hbm, k_other), (v_hbm, v_other))):
            loads.append(load_half(src, dst, False, sems.at[n, m], n * part, part))
    late = [load_half(src, dst, True, sems.at[2, m]) for m, (src, dst) in enumerate(((k_hbm, k_own), (v_hbm, v_own)))]
    quads = part // QUAD
    for n in range(2):
        wait_all(loads[2 * n : 2 * n + 2])
        states_of(k_other, v_other, send, range(n * quads, (n + 1) * quads))
    wait_all(late)


def second_kernel(k_own, v_own, q_hbm, gain_hbm, keep, q_own, q_other, gain, sems):
    loads = [load_half(q_hbm, q_own, True, sems.at[0]), load_half(q_hbm, q_other, False, sems.at[1])]
    loads.append(pltpu.make_async_copy(gain_hbm, gain, sems.at[2]))
    loads[-1].start()
    states_of(k_own, v_own, keep, range(k_own.shape[1] // QUAD))
    wait_all(loads)


def after_core(keep, got, *outs):
    state, other = keep[...], got[...].astype(F32)
    value = state + other
    ext = jnp.where(bit_of(0) == 0, state, other)
    rows = outs[0].shape[0]
    for n, (send, chip, ext_out) in enumerate((outs[:3], outs[3:])):
        part = value[n * rows : (n + 1) * rows]
        send[...] = part.astype(BF16)
        chip[...] = part
        ext_out[...] = ext[n * rows : (n + 1) * rows]


def low_first(chunk):
    return bit_of(0) == chunk


def with_got(before, got, chunk, n, rounds):
    value = got[...].astype(F32)
    taken = bit_of(1 + n)
    if n + 1 < rounds:
        taken = jnp.where(low_first(chunk), taken, bit_of(2 + n)) == 1
    else:
        taken = jnp.logical_or(taken == 1, jnp.logical_not(low_first(chunk)))
    value = jnp.where(taken, value, 0.0)
    return value if before is None else before[...] + value


def after_round(refs, *, chunk, n, rounds):
    refs = list(refs)
    before = refs.pop(0) if n else None
    total, got, *refs = refs
    sent = total[...] + got[...].astype(F32)
    value = with_got(before, got, chunk, n, rounds)
    if n + 2 == rounds:
        chip, send, before_out = refs
        share = value + jnp.where(bit_of(1) == 0, chip[...], 0.0)
        send[...] = jnp.where(low_first(chunk), sent, share).astype(BF16)
    else:
        send, before_out, total_out = refs
        send[...] = sent.astype(BF16)
        total_out[...] = sent
    before_out[...] = value


def after_last(before, got, ext, send, prior, *, chunk, n, rounds):
    base = with_got(before, got, chunk, n, rounds)
    ahead = base + ext[...]
    first = bit_of(0) == 0
    send[...] = jnp.where(first, ahead, base).astype(BF16)
    prior[...] = jnp.where(first, base, ahead).astype(BF16)


def intra_kernel(q_ref, k_ref, v_ref, intra_ref):
    count, half = intra_ref.shape
    mid = count // 2
    first = first_lanes((count, PAIR))
    rows = lax.broadcasted_iota(jnp.int32, (mid, mid), 0)
    cols = lax.broadcasted_iota(jnp.int32, (mid, mid), 1)
    causal = cols <= rows
    for p in range(half // PAIR):
        lanes = pl.ds(p * PAIR, PAIR)
        fq = jnp.maximum(q_ref[:, lanes], 0)
        fk = jnp.maximum(k_ref[:, lanes], 0)
        val = v_ref[:, lanes]
        zero = jnp.zeros_like(fq)
        top, low, weights = [], [], []
        for h in range(2):
            mine = first if h == 0 else jnp.logical_not(first)
            mine_q = jnp.where(mine, fq, zero)
            s_top = dot(mine_q[:mid], fk[:mid], ((1,), (1,)))
            s_low = dot(mine_q[mid:], fk, ((1,), (1,)))
            s_top = jnp.where(causal, s_top, 0.0).astype(BF16)
            s_diag = jnp.where(causal, s_low[:, mid:], 0.0).astype(BF16)
            s_low = jnp.concatenate([s_low[:, :mid].astype(BF16), s_diag], axis=1)
            top.append(s_top)
            low.append(s_low)
            weights.append(jnp.where(mine, val, zero))
        w_top = jnp.concatenate([w[:mid] for w in weights], axis=0)
        intra_ref[:mid, lanes] = dot(jnp.concatenate(top, axis=1), w_top, ((1,), (0,)))
        w_low = jnp.concatenate(weights, axis=0)
        intra_ref[mid:, lanes] = dot(jnp.concatenate(low, axis=1), w_low, ((1,), (0,)))


def final_kernel(refs, *, own, chunk, store, waiting, held):
    refs = list(refs)
    prior_ref, q_ref, gain_ref, intra_ref = refs[:4]
    left = refs[4 : 4 + len(waiting)]
    half = q_ref.shape[1]
    part = half // 2
    at = chunk * part
    base = half_start(own, half) + at
    copies = []
    if store:
        out_hbm, out, sems = refs[-3:]
        for n, ((other_own, other_chunk), src) in enumerate(zip(waiting, left)):
            there = pl.ds(pl.multiple_of(half_start(other_own, half) + other_chunk * part, part), part)
            copies.append(pltpu.make_async_copy(src, out_hbm.at[:, there], sems.at[1, n]))
            copies[-1].start()
    else:
        out = refs[-1]
    lane = lax.broadcasted_iota(jnp.int32, (QUAD, QUAD), 1) >> SHIFT
    row = lax.broadcasted_iota(jnp.int32, (QUAD, QUAD), 0) >> SHIFT
    same = lane == row
    ones = jnp.where(same, 1.0 / HEAD_DIM, 0.0).astype(BF16)
    numers = []
    for n in range(part // QUAD):
        one = prior_ref[pl.ds(n * PAIR, HEAD_DIM), :]
        two = prior_ref[pl.ds(n * PAIR + HEAD_DIM, HEAD_DIM), :]
        block = jnp.concatenate([jnp.concatenate([one, two], axis=1)] * 4, axis=0)
        block = jnp.where(same, block, jnp.zeros_like(block))
        lanes = pl.ds(at + n * QUAD, QUAD)
        fq = jnp.maximum(q_ref[:, lanes], 0)
        numers.append(dot(fq, block, ((1,), (0,))) + intra_ref[:, lanes])
    for n, numer in enumerate(numers):
        lanes = pl.ds(n * QUAD, QUAD)
        there = pl.ds(pl.multiple_of(base + n * QUAD, QUAD), QUAD)
        mean_sq = dot((numer * numer).astype(BF16), ones, ((1,), (0,)))
        out[:, lanes] = (numer * lax.rsqrt(mean_sq + EPS) * gain_ref[:, there]).astype(BF16)
        if store:
            copies.append(pltpu.make_async_copy(out.at[:, lanes], out_hbm.at[:, there], sems.at[0, n]))
            copies[-1].start()
    wait_all(copies)


ANY = pl.BlockSpec(memory_space=pl.ANY)
HBM = pl.BlockSpec(memory_space=pltpu.HBM)
VMEM = pl.BlockSpec(memory_space=pltpu.VMEM)
DMA = pltpu.SemaphoreType.DMA


def call(kernel, outs, args, specs=None, out_specs=None, scratch=(), alias=None, cost=(10_000, 10_000)):
    specs = [VMEM] * len(args) if specs is None else specs
    args = [a if s is ANY else pltpu.with_memory_space_constraint(a, s.memory_space) for a, s in zip(args, specs)]
    many = isinstance(outs, (tuple, list))
    return pl.pallas_call(
        kernel,
        out_shape=outs,
        in_specs=specs,
        out_specs=([VMEM] * len(outs) if many else VMEM) if out_specs is None else out_specs,
        scratch_shapes=scratch,
        input_output_aliases=alias or {},
        compiler_params=pltpu.CompilerParams(vmem_limit_bytes=12 * 2**20),
        cost_estimate=pl.CostEstimate(flops=cost[0], transcendentals=0, bytes_accessed=cost[1]),
    )(*args)


def packed(kernel, **static):
    return lambda *refs: kernel(refs, **static)


def on_device(queries, keys, values, gain, *, size):
    count, width = queries.shape
    half = width // 2
    rows = half // PAIR * HEAD_DIM
    rounds = size.bit_length() - 2
    tile = pltpu.VMEM((count, half), BF16)
    small16, small32 = pltpu.VMEM((rows, PAIR), BF16), pltpu.VMEM((rows, PAIR), F32)

    def swap(x, even, odd):
        return lax.ppermute(x, AXIS, [(i, i ^ (odd if i & CORE else even)) for i in range(size)])

    send, k_other, v_other, k_own, v_own = call(
        first_kernel, (small16, *[tile] * 4), (keys, values), specs=[HBM] * 2, scratch=[DMA((3, 2))]
    )
    got = swap(send, CORE, CORE)
    keep, q_own, q_other, gain_vmem = call(
        second_kernel,
        (small32, tile, tile, pltpu.VMEM((1, width), F32)),
        (k_own, v_own, queries, gain[None, :]),
        specs=[VMEM] * 2 + [HBM] * 2,
        scratch=[DMA((3,))],
        cost=(150_000_000, 2_000_000),
    )
    scores = pltpu.VMEM((count, half), F32)
    cost = (300_000_000, 2_000_000)
    intra_own = call(intra_kernel, scores, (q_own, k_own, v_own), cost=cost)
    intra_other = call(intra_kernel, scores, (q_other, k_other, v_other), cost=cost)

    part16, part32 = pltpu.VMEM((rows // 2, PAIR), BF16), pltpu.VMEM((rows // 2, PAIR), F32)
    outs = call(after_core, (part16, part32, part32) * 2, (keep, got))
    sends, chips, exts = ([outs[n], outs[n + 3]] for n in range(3))
    totals, befores, priors = list(chips), [None, None], [None, None]
    for n in range(rounds):
        low, high = SIDE << n, 2 << (n + 1) if n + 1 < rounds else SIDE
        gots = [swap(sends[c], *((low, high) if c == 0 else (high, low))) for c in range(2)]
        for c in range(2):
            static = {"chunk": c, "n": n, "rounds": rounds}
            before = [] if befores[c] is None else [befores[c]]
            if n + 1 == rounds:
                kernel = functools.partial(after_last, **static) if before else functools.partial(after_last, None, **static)
                sends[c], priors[c] = call(kernel, (part16, part16), [*before, gots[c], exts[c]])
                continue
            last = n + 2 == rounds
            sends[c], befores[c], *total = call(
                packed(after_round, **static),
                (part16, *[part32] * (1 if last else 2)),
                [*before, totals[c], gots[c], *([chips[c]] if last else [])],
            )
            totals[c] = total[0] if total else None
    gots = [swap(sends[c], CORE, CORE) for c in range(2)]

    out_tile = pltpu.VMEM((count, half // 2), BF16)
    inputs = {True: (q_own, gain_vmem, intra_own), False: (q_other, gain_vmem, intra_other)}
    out, waiting, left = None, [], []
    for own, c in ((True, 0), (False, 0), (True, 1), (False, 1)):
        store = c == 1
        args = [priors[c] if own else gots[c], *inputs[own], *left]
        specs = [VMEM] * len(args)
        held = out is not None
        if held:
            args, specs = [*args, out], [*specs, ANY]
        result = call(
            packed(final_kernel, own=own, chunk=c, store=store, waiting=tuple(waiting) if left else (), held=held),
            jax.ShapeDtypeStruct((count, width), BF16) if store else out_tile,
            args,
            specs=specs,
            out_specs=ANY if store else None,
            scratch=[out_tile, DMA((2, 2))] if store else (),
            alias={len(args) - 1: 0} if held else {},
            cost=(100_000_000, 1_000_000),
        )
        if store:
            out, left, waiting = result, [], []
        else:
            waiting.append((own, c))
            pending = [*pending, result] if len(waiting) > 1 else [result]
            if len(waiting) == 2:
                left = pending
    return out


def solution(mesh):
    return jax.shard_map(
        functools.partial(on_device, size=mesh.shape[AXIS]),
        mesh=mesh,
        in_specs=(
            P(("groups", "seq"), None),
            P(("groups", "seq"), None),
            P(("groups", "seq"), None),
            P(),
        ),
        out_specs=P(("groups", "seq"), None),
        check_vma=False,
    )
```

```python
import functools

import jax
import jax.numpy as jnp
from jax import lax
from jax.experimental import pallas as pl
from jax.experimental.pallas import tpu as pltpu
from jax.sharding import PartitionSpec as P


HEAD_DIM = 64
PAIR = 2 * HEAD_DIM
QUAD = 4 * HEAD_DIM
SHIFT = 6
CORE, SIDE = 1, 2
BLOCKS = 2
EPS = 1e-05
AXIS = "seq"
BF16, F32 = jnp.bfloat16, jnp.float32


def bit_of(level):
    return (lax.axis_index(AXIS) >> level) & 1


def first_lanes(shape):
    return lax.broadcasted_iota(jnp.int32, shape, len(shape) - 1) < HEAD_DIM


def dot(a, b, dims):
    return lax.dot_general(a, b, (dims, ((), ())), preferred_element_type=F32)


def half_start(own, half):
    core = bit_of(0)
    return pl.multiple_of((core if own else 1 - core) * half, half)


def load_half(src, dst, own, sem, start=0, width=None):
    half = dst.shape[1]
    width = half if width is None else width
    there = pl.ds(pl.multiple_of(half_start(own, half) + start, width), width)
    load = pltpu.make_async_copy(src.at[:, there], dst.at[:, pl.ds(start, width)], sem)
    load.start()
    return load


def wait_all(loads):
    for load in loads:
        load.wait()


def states_of(k_ref, v_ref, out_ref, quads):
    first = first_lanes((HEAD_DIM, PAIR))
    for quad in quads:
        lanes = pl.ds(quad * QUAD, QUAD)
        fk = jnp.maximum(k_ref[:, lanes], 0)
        full = dot(fk, v_ref[:, lanes], ((0,), (0,)))
        for p in range(2):
            top = p * PAIR
            rows = full[top : top + PAIR, top : top + PAIR]
            packed = jnp.where(first, rows[:HEAD_DIM], rows[HEAD_DIM:])
            out_ref[pl.ds((quad * 2 + p) * HEAD_DIM, HEAD_DIM), :] = packed.astype(out_ref.dtype)


def first_kernel(k_hbm, v_hbm, send, k_other, v_other, k_own, v_own, sems):
    half = k_other.shape[1]
    part = half // 2
    loads = []
    for n in range(2):
        for m, (src, dst) in enumerate(((k_hbm, k_other), (v_hbm, v_other))):
            loads.append(load_half(src, dst, False, sems.at[n, m], n * part, part))
    late = [load_half(src, dst, True, sems.at[2, m]) for m, (src, dst) in enumerate(((k_hbm, k_own), (v_hbm, v_own)))]
    quads = part // QUAD
    for n in range(2):
        wait_all(loads[2 * n : 2 * n + 2])
        states_of(k_other, v_other, send, range(n * quads, (n + 1) * quads))
    wait_all(late)


def second_kernel(k_own, v_own, q_hbm, gain_hbm, keep, q_own, q_other, gain, sems):
    loads = [load_half(q_hbm, q_own, True, sems.at[0]), load_half(q_hbm, q_other, False, sems.at[1])]
    loads.append(pltpu.make_async_copy(gain_hbm, gain, sems.at[2]))
    loads[-1].start()
    states_of(k_own, v_own, keep, range(k_own.shape[1] // QUAD))
    wait_all(loads)


def after_core(keep, got, send, total, ext):
    state, other = keep[...], got[...].astype(F32)
    value = state + other
    send[...] = value.astype(BF16)
    total[...] = value
    ext[...] = jnp.where(bit_of(0) == 0, state, other)


def later_of(n, rounds):
    low = bit_of(1 + n)
    return jnp.where(bit_of(0) == 0, low, bit_of(2 + n)) if n + 1 < rounds else low


def with_got(before, got, n, rounds):
    value = got[...].astype(F32)
    taken = later_of(n, rounds) == 1
    if n + 1 == rounds:
        taken = jnp.logical_or(taken, bit_of(0) == 1)
    value = jnp.where(taken, value, 0.0)
    return value if before is None else before[...] + value


def after_round(refs, *, n, rounds):
    refs = list(refs)
    before = refs.pop(0) if n else None
    total, got, *refs = refs
    sent = total[...] + got[...].astype(F32)
    value = with_got(before, got, n, rounds)
    if n + 2 == rounds:
        chip, send, before_out = refs
        share = value + jnp.where(bit_of(1) == 0, chip[...], 0.0)
        send[...] = jnp.where(bit_of(0) == 0, sent, share).astype(BF16)
    else:
        send, before_out, total_out = refs
        send[...] = sent.astype(BF16)
        total_out[...] = sent
    before_out[...] = value


def after_last(before, got, ext, send, prior, *, n, rounds):
    base = with_got(before, got, n, rounds)
    ahead = base + ext[...]
    first = bit_of(0) == 0
    send[...] = jnp.where(first, ahead, base).astype(BF16)
    prior[...] = jnp.where(first, base, ahead).astype(BF16)


def intra_kernel(q_ref, k_ref, v_ref, intra_ref):
    count, half = intra_ref.shape
    mid = count // 2
    first = first_lanes((count, PAIR))
    rows = lax.broadcasted_iota(jnp.int32, (mid, mid), 0)
    cols = lax.broadcasted_iota(jnp.int32, (mid, mid), 1)
    causal = cols <= rows
    for p in range(half // PAIR):
        lanes = pl.ds(p * PAIR, PAIR)
        fq = jnp.maximum(q_ref[:, lanes], 0)
        fk = jnp.maximum(k_ref[:, lanes], 0)
        val = v_ref[:, lanes]
        zero = jnp.zeros_like(fq)
        top, low, weights = [], [], []
        for h in range(2):
            mine = first if h == 0 else jnp.logical_not(first)
            mine_q = jnp.where(mine, fq, zero)
            s_top = dot(mine_q[:mid], fk[:mid], ((1,), (1,)))
            s_low = dot(mine_q[mid:], fk, ((1,), (1,)))
            s_top = jnp.where(causal, s_top, 0.0).astype(BF16)
            s_diag = jnp.where(causal, s_low[:, mid:], 0.0).astype(BF16)
            s_low = jnp.concatenate([s_low[:, :mid].astype(BF16), s_diag], axis=1)
            top.append(s_top)
            low.append(s_low)
            weights.append(jnp.where(mine, val, zero))
        w_top = jnp.concatenate([w[:mid] for w in weights], axis=0)
        intra_ref[:mid, lanes] = dot(jnp.concatenate(top, axis=1), w_top, ((1,), (0,)))
        w_low = jnp.concatenate(weights, axis=0)
        intra_ref[mid:, lanes] = dot(jnp.concatenate(low, axis=1), w_low, ((1,), (0,)))


def final_kernel(refs, *, own):
    prior_ref, q_ref, gain_ref, intra_ref = refs[:4]
    out_hbm, out_buf, sems = refs[-3:]
    half = out_buf.shape[1]
    base = half_start(own, half)
    lane = lax.broadcasted_iota(jnp.int32, (QUAD, QUAD), 1) >> SHIFT
    row = lax.broadcasted_iota(jnp.int32, (QUAD, QUAD), 0) >> SHIFT
    same = lane == row
    ones = jnp.where(same, 1.0 / HEAD_DIM, 0.0).astype(BF16)
    copies = []

    def numer_of(n):
        one = prior_ref[pl.ds(n * PAIR, HEAD_DIM), :]
        two = prior_ref[pl.ds(n * PAIR + HEAD_DIM, HEAD_DIM), :]
        block = jnp.concatenate([jnp.concatenate([one, two], axis=1)] * 4, axis=0)
        block = jnp.where(same, block, jnp.zeros_like(block))
        lanes = pl.ds(n * QUAD, QUAD)
        fq = jnp.maximum(q_ref[:, lanes], 0)
        return dot(fq, block, ((1,), (0,))) + intra_ref[:, lanes]

    quads = half // QUAD
    numers = [numer_of(n) for n in range(quads)]
    means = [dot((numer * numer).astype(BF16), ones, ((1,), (0,))) for numer in numers]
    count = q_ref.shape[0]
    rows = count // BLOCKS
    for n in range(quads):
        lanes = pl.ds(n * QUAD, QUAD)
        there = pl.ds(pl.multiple_of(base + n * QUAD, QUAD), QUAD)
        gain = gain_ref[:, there]
        for m in range(BLOCKS):
            tokens = pl.ds(m * rows, rows)
            numer, mean_sq = (x[n][m * rows : (m + 1) * rows] for x in (numers, means))
            out_buf[tokens, lanes] = (numer * lax.rsqrt(mean_sq + EPS) * gain).astype(BF16)
            copies.append(
                pltpu.make_async_copy(out_buf.at[tokens, lanes], out_hbm.at[tokens, there], sems.at[n, m])
            )
            copies[-1].start()
    wait_all(copies)


ANY = pl.BlockSpec(memory_space=pl.ANY)
HBM = pl.BlockSpec(memory_space=pltpu.HBM)
VMEM = pl.BlockSpec(memory_space=pltpu.VMEM)
DMA = pltpu.SemaphoreType.DMA


def call(kernel, outs, args, specs=None, out_specs=None, scratch=(), alias=None, cost=(10_000, 10_000)):
    specs = [VMEM] * len(args) if specs is None else specs
    args = [a if s is ANY else pltpu.with_memory_space_constraint(a, s.memory_space) for a, s in zip(args, specs)]
    many = isinstance(outs, (tuple, list))
    return pl.pallas_call(
        kernel,
        out_shape=outs,
        in_specs=specs,
        out_specs=([VMEM] * len(outs) if many else VMEM) if out_specs is None else out_specs,
        scratch_shapes=scratch,
        input_output_aliases=alias or {},
        compiler_params=pltpu.CompilerParams(vmem_limit_bytes=12 * 2**20),
        cost_estimate=pl.CostEstimate(flops=cost[0], transcendentals=0, bytes_accessed=cost[1]),
    )(*args)


def packed(kernel, **static):
    return lambda *refs: kernel(refs, **static)


def on_device(queries, keys, values, gain, *, size):
    count, width = queries.shape
    half = width // 2
    rows = half // PAIR * HEAD_DIM
    rounds = size.bit_length() - 2
    tile = pltpu.VMEM((count, half), BF16)
    small16, small32 = pltpu.VMEM((rows, PAIR), BF16), pltpu.VMEM((rows, PAIR), F32)

    def swap(x, even, odd):
        return lax.ppermute(x, AXIS, [(i, i ^ (odd if i & CORE else even)) for i in range(size)])

    send, k_other, v_other, k_own, v_own = call(
        first_kernel, (small16, *[tile] * 4), (keys, values), specs=[HBM] * 2, scratch=[DMA((3, 2))]
    )
    got = swap(send, CORE, CORE)
    keep, q_own, q_other, gain_vmem = call(
        second_kernel,
        (small32, tile, tile, pltpu.VMEM((1, width), F32)),
        (k_own, v_own, queries, gain[None, :]),
        specs=[VMEM] * 2 + [HBM] * 2,
        scratch=[DMA((3,))],
        cost=(150_000_000, 2_000_000),
    )
    scores = pltpu.VMEM((count, half), F32)
    cost = (300_000_000, 2_000_000)
    intra_own = call(intra_kernel, scores, (q_own, k_own, v_own), cost=cost)
    intra_other = call(intra_kernel, scores, (q_other, k_other, v_other), cost=cost)

    send, chip, ext = call(after_core, (small16, small32, small32), (keep, got))
    total, before = chip, []
    for n in range(rounds):
        odd = 2 << (n + 1) if n + 1 < rounds else SIDE
        got = swap(send, SIDE << n, odd)
        if n + 1 == rounds:
            break
        last = n + 2 == rounds
        send, *before = call(
            packed(after_round, n=n, rounds=rounds),
            (small16, *[small32] * (1 if last else 2)),
            [*before[:1], total, got, *([chip] if last else [])],
        )
        if not last:
            total = before.pop()
    send, prior = call(
        functools.partial(after_last, n=rounds - 1, rounds=rounds), (small16, small16), [*before, got, ext]
    )
    got = swap(send, CORE, CORE)

    out = None
    for own, prior, q, intra in ((True, prior, q_own, intra_own), (False, got, q_other, intra_other)):
        args = [prior, q, gain_vmem, intra]
        specs = [VMEM] * 4
        alias = {}
        if out is not None:
            args, specs, alias = [*args, out], [*specs, ANY], {4: 0}
        out = call(
            packed(final_kernel, own=own),
            jax.ShapeDtypeStruct((count, width), BF16),
            args,
            specs=specs,
            out_specs=ANY,
            scratch=[tile, DMA((half // QUAD, BLOCKS))],
            alias=alias,
            cost=(100_000_000, 2_000_000),
        )
    return out


def solution(mesh):
    return jax.shard_map(
        functools.partial(on_device, size=mesh.shape[AXIS]),
        mesh=mesh,
        in_specs=(
            P(("groups", "seq"), None),
            P(("groups", "seq"), None),
            P(("groups", "seq"), None),
            P(),
        ),
        out_specs=P(("groups", "seq"), None),
        check_vma=False,
    )
```

```python
import functools

import jax
import jax.numpy as jnp
from jax import lax
from jax.experimental import pallas as pl
from jax.experimental.pallas import tpu as pltpu
from jax.sharding import PartitionSpec as P


HEAD_DIM = 64
PAIR = 2 * HEAD_DIM
QUAD = 4 * HEAD_DIM
SHIFT = 6
CORE, SIDE = 1, 2
BLOCKS = 2
EPS = 1e-05
AXIS = "seq"
BF16, F32 = jnp.bfloat16, jnp.float32


def bit_of(level):
    return (lax.axis_index(AXIS) >> level) & 1


def first_lanes(shape):
    return lax.broadcasted_iota(jnp.int32, shape, len(shape) - 1) < HEAD_DIM


def dot(a, b, dims):
    return lax.dot_general(a, b, (dims, ((), ())), preferred_element_type=F32)


def half_start(own, half):
    core = bit_of(0)
    return pl.multiple_of((core if own else 1 - core) * half, half)


def load_half(src, dst, own, sem, start=0, width=None):
    half = dst.shape[1]
    width = half if width is None else width
    there = pl.ds(pl.multiple_of(half_start(own, half) + start, width), width)
    load = pltpu.make_async_copy(src.at[:, there], dst.at[:, pl.ds(start, width)], sem)
    load.start()
    return load


def wait_all(loads):
    for load in loads:
        load.wait()


def states_of(k_ref, v_ref, out_ref, quads):
    first = first_lanes((HEAD_DIM, PAIR))
    for quad in quads:
        lanes = pl.ds(quad * QUAD, QUAD)
        fk = jnp.maximum(k_ref[:, lanes], 0)
        full = dot(fk, v_ref[:, lanes], ((0,), (0,)))
        for p in range(2):
            top = p * PAIR
            rows = full[top : top + PAIR, top : top + PAIR]
            packed = jnp.where(first, rows[:HEAD_DIM], rows[HEAD_DIM:])
            out_ref[pl.ds((quad * 2 + p) * HEAD_DIM, HEAD_DIM), :] = packed.astype(out_ref.dtype)


def first_kernel(k_hbm, v_hbm, send, k_other, v_other, k_own, v_own, turned, sems):
    loads = []
    for own, k_ref, v_ref in ((False, k_other, v_other), (True, k_own, v_own)):
        for src, dst in ((k_hbm, k_ref), (v_hbm, v_ref)):
            loads.append(load_half(src, dst, own, sems.at[len(loads)]))
    first = first_lanes((HEAD_DIM, PAIR))
    quads = k_other.shape[1] // QUAD
    loads[0].wait()
    for quad in range(quads):
        lanes = pl.ds(quad * QUAD, QUAD)
        turned[lanes, :] = jnp.transpose(jnp.maximum(k_other[:, lanes], 0))
    loads[1].wait()
    for quad in range(quads):
        lanes = pl.ds(quad * QUAD, QUAD)
        full = dot(turned[lanes, :], v_other[:, lanes], ((1,), (0,)))
        for p in range(2):
            top = p * PAIR
            rows = full[top : top + PAIR, top : top + PAIR]
            packed = jnp.where(first, rows[:HEAD_DIM], rows[HEAD_DIM:])
            send[pl.ds((quad * 2 + p) * HEAD_DIM, HEAD_DIM), :] = packed.astype(send.dtype)
    wait_all(loads[2:])


def second_kernel(k_own, v_own, q_hbm, gain_hbm, keep, q_own, q_other, gain, sems):
    loads = [load_half(q_hbm, q_own, True, sems.at[0]), load_half(q_hbm, q_other, False, sems.at[1])]
    loads.append(pltpu.make_async_copy(gain_hbm, gain, sems.at[2]))
    loads[-1].start()
    states_of(k_own, v_own, keep, range(k_own.shape[1] // QUAD))
    wait_all(loads)


def after_core(keep, got, send, total, ext):
    state, other = keep[...], got[...].astype(F32)
    value = state + other
    send[...] = value.astype(BF16)
    total[...] = value
    ext[...] = jnp.where(bit_of(0) == 0, state, other)


def later_of(n, rounds):
    low = bit_of(1 + n)
    return jnp.where(bit_of(0) == 0, low, bit_of(2 + n)) if n + 1 < rounds else low


def with_got(before, got, n, rounds):
    value = got[...].astype(F32)
    taken = later_of(n, rounds) == 1
    if n + 1 == rounds:
        taken = jnp.logical_or(taken, bit_of(0) == 1)
    value = jnp.where(taken, value, 0.0)
    return value if before is None else before[...] + value


def after_round(refs, *, n, rounds):
    refs = list(refs)
    before = refs.pop(0) if n else None
    total, got, *refs = refs
    sent = total[...] + got[...].astype(F32)
    value = with_got(before, got, n, rounds)
    if n + 2 == rounds:
        chip, send, before_out = refs
        share = value + jnp.where(bit_of(1) == 0, chip[...], 0.0)
        send[...] = jnp.where(bit_of(0) == 0, sent, share).astype(BF16)
    else:
        send, before_out, total_out = refs
        send[...] = sent.astype(BF16)
        total_out[...] = sent
    before_out[...] = value


def after_last(before, got, ext, send, prior, *, n, rounds):
    base = with_got(before, got, n, rounds)
    ahead = base + ext[...]
    first = bit_of(0) == 0
    send[...] = jnp.where(first, ahead, base).astype(BF16)
    prior[...] = jnp.where(first, base, ahead).astype(BF16)


def intra_kernel(q_ref, k_ref, v_ref, intra_ref):
    count, half = intra_ref.shape
    mid = count // 2
    first = first_lanes((count, PAIR))
    rows = lax.broadcasted_iota(jnp.int32, (mid, mid), 0)
    cols = lax.broadcasted_iota(jnp.int32, (mid, mid), 1)
    causal = cols <= rows
    for p in range(half // PAIR):
        lanes = pl.ds(p * PAIR, PAIR)
        fq = jnp.maximum(q_ref[:, lanes], 0)
        fk = jnp.maximum(k_ref[:, lanes], 0)
        val = v_ref[:, lanes]
        zero = jnp.zeros_like(fq)
        top, low, weights = [], [], []
        for h in range(2):
            mine = first if h == 0 else jnp.logical_not(first)
            mine_q = jnp.where(mine, fq, zero)
            s_top = dot(mine_q[:mid], fk[:mid], ((1,), (1,)))
            s_low = dot(mine_q[mid:], fk, ((1,), (1,)))
            s_top = jnp.where(causal, s_top, 0.0).astype(BF16)
            s_diag = jnp.where(causal, s_low[:, mid:], 0.0).astype(BF16)
            s_low = jnp.concatenate([s_low[:, :mid].astype(BF16), s_diag], axis=1)
            top.append(s_top)
            low.append(s_low)
            weights.append(jnp.where(mine, val, zero))
        w_top = jnp.concatenate([w[:mid] for w in weights], axis=0)
        intra_ref[:mid, lanes] = dot(jnp.concatenate(top, axis=1), w_top, ((1,), (0,)))
        w_low = jnp.concatenate(weights, axis=0)
        intra_ref[mid:, lanes] = dot(jnp.concatenate(low, axis=1), w_low, ((1,), (0,)))


def final_kernel(refs, *, own):
    prior_ref, q_ref, gain_ref, intra_ref = refs[:4]
    out_hbm, out_buf, sems = refs[-3:]
    half = out_buf.shape[1]
    base = half_start(own, half)
    lane = lax.broadcasted_iota(jnp.int32, (QUAD, QUAD), 1) >> SHIFT
    row = lax.broadcasted_iota(jnp.int32, (QUAD, QUAD), 0) >> SHIFT
    same = lane == row
    ones = jnp.where(same, 1.0 / HEAD_DIM, 0.0).astype(BF16)
    copies = []

    def numer_of(n):
        one = prior_ref[pl.ds(n * PAIR, HEAD_DIM), :]
        two = prior_ref[pl.ds(n * PAIR + HEAD_DIM, HEAD_DIM), :]
        block = jnp.concatenate([jnp.concatenate([one, two], axis=1)] * 4, axis=0)
        block = jnp.where(same, block, jnp.zeros_like(block))
        lanes = pl.ds(n * QUAD, QUAD)
        fq = jnp.maximum(q_ref[:, lanes], 0)
        return dot(fq, block, ((1,), (0,))) + intra_ref[:, lanes]

    quads = half // QUAD
    numers = [numer_of(n) for n in range(quads)]
    means = [dot((numer * numer).astype(BF16), ones, ((1,), (0,))) for numer in numers]
    count = q_ref.shape[0]
    rows = count // BLOCKS
    for n in range(quads):
        lanes = pl.ds(n * QUAD, QUAD)
        there = pl.ds(pl.multiple_of(base + n * QUAD, QUAD), QUAD)
        gain = gain_ref[:, there]
        for m in range(BLOCKS):
            tokens = pl.ds(m * rows, rows)
            numer, mean_sq = (x[n][m * rows : (m + 1) * rows] for x in (numers, means))
            out_buf[tokens, lanes] = (numer * lax.rsqrt(mean_sq + EPS) * gain).astype(BF16)
            copies.append(
                pltpu.make_async_copy(out_buf.at[tokens, lanes], out_hbm.at[tokens, there], sems.at[n, m])
            )
            copies[-1].start()
    wait_all(copies)


ANY = pl.BlockSpec(memory_space=pl.ANY)
HBM = pl.BlockSpec(memory_space=pltpu.HBM)
VMEM = pl.BlockSpec(memory_space=pltpu.VMEM)
DMA = pltpu.SemaphoreType.DMA


def call(kernel, outs, args, specs=None, out_specs=None, scratch=(), alias=None, cost=(10_000, 10_000)):
    specs = [VMEM] * len(args) if specs is None else specs
    args = [a if s is ANY else pltpu.with_memory_space_constraint(a, s.memory_space) for a, s in zip(args, specs)]
    many = isinstance(outs, (tuple, list))
    return pl.pallas_call(
        kernel,
        out_shape=outs,
        in_specs=specs,
        out_specs=([VMEM] * len(outs) if many else VMEM) if out_specs is None else out_specs,
        scratch_shapes=scratch,
        input_output_aliases=alias or {},
        compiler_params=pltpu.CompilerParams(vmem_limit_bytes=12 * 2**20),
        cost_estimate=pl.CostEstimate(flops=cost[0], transcendentals=0, bytes_accessed=cost[1]),
    )(*args)


def packed(kernel, **static):
    return lambda *refs: kernel(refs, **static)


def on_device(queries, keys, values, gain, *, size):
    count, width = queries.shape
    half = width // 2
    rows = half // PAIR * HEAD_DIM
    rounds = size.bit_length() - 2
    tile = pltpu.VMEM((count, half), BF16)
    small16, small32 = pltpu.VMEM((rows, PAIR), BF16), pltpu.VMEM((rows, PAIR), F32)

    def swap(x, even, odd):
        return lax.ppermute(x, AXIS, [(i, i ^ (odd if i & CORE else even)) for i in range(size)])

    send, k_other, v_other, k_own, v_own = call(
        first_kernel, (small16, *[tile] * 4), (keys, values), specs=[HBM] * 2, scratch=[pltpu.VMEM((half, count), BF16), DMA((4,))]
    )
    got = swap(send, CORE, CORE)
    keep, q_own, q_other, gain_vmem = call(
        second_kernel,
        (small32, tile, tile, pltpu.VMEM((1, width), F32)),
        (k_own, v_own, queries, gain[None, :]),
        specs=[VMEM] * 2 + [HBM] * 2,
        scratch=[DMA((3,))],
        cost=(150_000_000, 2_000_000),
    )
    scores = pltpu.VMEM((count, half), F32)
    cost = (300_000_000, 2_000_000)
    intra_own = call(intra_kernel, scores, (q_own, k_own, v_own), cost=cost)
    intra_other = call(intra_kernel, scores, (q_other, k_other, v_other), cost=cost)

    send, chip, ext = call(after_core, (small16, small32, small32), (keep, got))
    total, before = chip, []
    for n in range(rounds):
        odd = 2 << (n + 1) if n + 1 < rounds else SIDE
        got = swap(send, SIDE << n, odd)
        if n + 1 == rounds:
            break
        last = n + 2 == rounds
        send, *before = call(
            packed(after_round, n=n, rounds=rounds),
            (small16, *[small32] * (1 if last else 2)),
            [*before[:1], total, got, *([chip] if last else [])],
        )
        if not last:
            total = before.pop()
    send, prior = call(
        functools.partial(after_last, n=rounds - 1, rounds=rounds), (small16, small16), [*before, got, ext]
    )
    got = swap(send, CORE, CORE)

    out = None
    for own, prior, q, intra in ((True, prior, q_own, intra_own), (False, got, q_other, intra_other)):
        args = [prior, q, gain_vmem, intra]
        specs = [VMEM] * 4
        alias = {}
        if out is not None:
            args, specs, alias = [*args, out], [*specs, ANY], {4: 0}
        out = call(
            packed(final_kernel, own=own),
            jax.ShapeDtypeStruct((count, width), BF16),
            args,
            specs=specs,
            out_specs=ANY,
            scratch=[tile, DMA((half // QUAD, BLOCKS))],
            alias=alias,
            cost=(100_000_000, 2_000_000),
        )
    return out


def solution(mesh):
    return jax.shard_map(
        functools.partial(on_device, size=mesh.shape[AXIS]),
        mesh=mesh,
        in_specs=(
            P(("groups", "seq"), None),
            P(("groups", "seq"), None),
            P(("groups", "seq"), None),
            P(),
        ),
        out_specs=P(("groups", "seq"), None),
        check_vma=False,
    )
```
